32 devices in a mesh: pipe: 4 (over y, x), tensor: 2 (over core), dp: 4 (over z).
Axes of the slice: x: 2, y: 2, z: 4, core: 2. Of those that a mesh axis runs over, the one named last changes fastest.
Arguments:
- x_fwd: bfloat16 [4, 4, 96, 4096], P('pipe', 'dp', 'tensor'), may hold values from -6 to 6
- x_bwd: bfloat16 [4, 4, 96, 4096], P('pipe', 'dp', 'tensor'), may hold values from -6 to 6
- grad_out: bfloat16 [4, 4, 96, 4096], P('pipe', 'dp', 'tensor'), may hold values from -6 to 6
- saved_qkv: bfloat16 [4, 4, 96, 6144], P('pipe', 'dp', None, 'tensor'), may hold values from -32 to 32
- norm_gain: float32 [4, 4096], P('pipe'), may hold values from 0.5 to 1.5
- w_qkv: bfloat16 [4, 4096, 6144], P('pipe', None, 'tensor'), may hold values from -8 to 8
- w_out: bfloat16 [4, 4608, 4096], P('pipe', 'tensor', 'dp'), may hold values from -0.09375 to 0.09375
Outputs:
- next_input: bfloat16 [4, 4, 96, 4096], P('pipe', 'dp', 'tensor')
- prev_grad: bfloat16 [4, 4, 96, 4096], P('pipe', 'dp', 'tensor')
The draws below stay inside these ranges and needn't reach their ends.
All inputs are finite; a program needn't handle non-finite values.
Results may differ from the reference program's by a relative error of at most 0.019.
Values may be sent and summed in bfloat16 or wider, within the bound.
No kernel may reach another device: no remote copies, remote signals or barrier semaphores. Data moves between devices by JAX's collectives and lax.ppermute only.
A program may use at most 64 MiB of HBM per device.

```python
import math
import jax
import jax.numpy as jnp
from jax import lax

D = 4096
HD = 128
KVH = 6
GROUP = 6
HEADS = 36
TOK = 96
N_PIPE = 4
N_TENSOR = 2
N_DP = 4


def draw_x_fwd(key, part):
    base_key = jax.random.fold_in(jax.random.fold_in(key, 11), 0)
    shape = (N_PIPE, N_DP, TOK, D)
    field = jnp.clip(jax.random.normal(base_key, shape, jnp.float32), -6.0, 6.0)
    position = lax.broadcasted_iota(jnp.int32, (1, 1, TOK, 1), 2)
    feature = lax.broadcasted_iota(jnp.int32, (1, 1, 1, D), 3)
    earlier = jnp.concatenate([field[:, :, :1], field[:, :, :-1]], axis=2)
    copied = (position % 8 == 1) & (feature < D // 2)
    return jnp.where(copied, earlier, field).astype(jnp.bfloat16)


def draw_w_qkv(key, part):
    section_root = jax.random.fold_in(key, 23)

    def one_section(section):
        drawn_key, common_key, pick_key, power_key = jax.random.split(jax.random.fold_in(section_root, section), 4)
        shape = (D, KVH, GROUP + 2, HD)
        common_shape = (D, KVH, 1, HD)
        drawn = jnp.clip(jax.random.normal(drawn_key, shape, jnp.float32), -4.0, 4.0)
        common = jnp.clip(jax.random.normal(common_key, common_shape, jnp.float32), -4.0, 4.0)
        drawn = drawn / math.sqrt(D)
        feature = lax.broadcasted_iota(jnp.int32, (D, 1, 1, 1), 0)
        target = jnp.exp(jax.random.uniform(power_key, (1, KVH, 1, 1), jnp.float32, math.log(100.0), math.log(350.0)))
        strength = jnp.sqrt(target / math.sqrt(HD)) * math.sqrt(2.0 / D)
        common = jnp.where(feature < D // 2, common * strength, 0.0)
        chosen = jax.random.randint(pick_key, (1, KVH, 1, 1), 0, GROUP)
        slot = lax.broadcasted_iota(jnp.int32, (1, 1, GROUP + 2, 1), 2)
        linked = (slot == chosen) | (slot == GROUP)
        joined = jnp.where(linked, common, drawn)
        return joined.reshape(D, KVH * (GROUP + 2) * HD).astype(jnp.bfloat16)
    return lax.map(one_section, jnp.arange(N_PIPE, dtype=jnp.int32))


def draw_saved_qkv(key, part):
    drawn_key, power_key, pick_key, gap_key, anchor_key = jax.random.split(jax.random.fold_in(key, 37), 5)
    shape = (N_PIPE, N_DP, TOK, KVH, GROUP + 2, HD)
    drawn = jnp.clip(jax.random.normal(drawn_key, shape, jnp.float32), -4.0, 4.0)
    row_shape = (N_PIPE, N_DP, TOK, KVH, 1)
    position = lax.broadcasted_iota(jnp.int32, (1, 1, TOK, 1, 1), 2)
    key_drawn = drawn[:, :, :, :, GROUP]
    target = jnp.exp(jax.random.uniform(power_key, row_shape, jnp.float32, math.log(100.0), math.log(350.0)))
    strength = jnp.sqrt(target / math.sqrt(HD))
    scaled = key_drawn * strength
    energy = jnp.sum(scaled * scaled, axis=-1, keepdims=True) / math.sqrt(HD)
    gap = jax.random.uniform(gap_key, row_shape, jnp.float32, 1.0, 3.0)
    twin = scaled * (1.0 + gap / energy)
    twin_prior = jnp.concatenate([twin[:, :, :1], twin[:, :, :-1]], axis=2)
    phase = position % 8
    key_rows = jnp.where(phase == 0, scaled, jnp.where(phase == 1, twin_prior, key_drawn))
    upper = position[:, :, :, :, 0] // 8 + 1
    anchor = 8 * jax.random.randint(anchor_key, (N_PIPE, N_DP, TOK, KVH), 0, upper)
    anchor_full = jnp.broadcast_to(anchor[:, :, :, :, None], (N_PIPE, N_DP, TOK, KVH, HD))
    picked = jnp.take_along_axis(key_rows, anchor_full, axis=2)
    chosen = jax.random.randint(pick_key, (N_PIPE, N_DP, 1, KVH, 1, 1), 0, GROUP)
    slot = lax.broadcasted_iota(jnp.int32, (1, 1, 1, 1, GROUP + 2, 1), 4)
    query_rows = (slot == chosen) & (position[:, :, :, :, :, None] % 8 == 4)
    joined = jnp.where(slot == GROUP, key_rows[:, :, :, :, None], drawn)
    joined = jnp.where(query_rows, picked[:, :, :, :, None], joined)
    joined = jnp.clip(joined, -32.0, 32.0)
    return joined.reshape(N_PIPE, N_DP, TOK, KVH * (GROUP + 2) * HD).astype(jnp.bfloat16)


def levels(stream_key, dims, cuts, smallest, largest):
    level, own = 1.0, jax.random.fold_in(stream_key, 6)
    for dim, blocks in cuts:
        heights = jnp.exp(jax.random.uniform(jax.random.fold_in(own, dim), (blocks,), jnp.float32, smallest / len(cuts), largest / len(cuts)))
        level = level * jnp.repeat(heights, dims[dim] // blocks).reshape([-1 if axis == dim else 1 for axis in range(len(dims))])
    return level


def bell_draw(rng, extent, deviation, bound, pieces=(), kind=jnp.bfloat16):
    entries = jax.random.normal(rng, extent, jnp.float32) * deviation
    if len(pieces) > 0:
        entries = levels(rng, extent, pieces, -0.22, 0.18) * entries
    return jnp.clip(entries, min=-bound, max=bound).astype(kind)


def setup_inputs(seed: int = 0) -> dict:
    key_of = jax.random.split(jax.random.key(seed), 8)
    return {
        "x_fwd": draw_x_fwd(jax.random.fold_in(key_of[7], 71), 0),
        "x_bwd": bell_draw(key_of[1], (N_PIPE, N_DP, TOK, D), 1.0, 6.0, ((0, 4), (1, 4), (2, 2))),
        "grad_out": bell_draw(key_of[2], (N_PIPE, N_DP, TOK, D), 1.0, 6.0, ((0, 4), (1, 4), (2, 2))),
        "saved_qkv": draw_saved_qkv(jax.random.fold_in(key_of[7], 71), 0),
        "norm_gain": jnp.clip(1.0 + 0.1 * jax.random.normal(key_of[4], (N_PIPE, D), jnp.float32), 0.5, 1.5),
        "w_qkv": draw_w_qkv(jax.random.fold_in(key_of[7], 71), 0),
        "w_out": bell_draw(key_of[6], (N_PIPE, HEADS * HD, D), (HEADS * HD) ** -0.5, 0.09375, ((0, 4), (1, 2), (2, 4))),
    }


def normalize(inputs, gain_row):
    widened = inputs.astype(jnp.float32)
    inverse = lax.rsqrt(lax.optimization_barrier(jnp.mean(widened * widened, axis=-1, keepdims=True)) + 1e-05)
    return (widened * inverse * gain_row).astype(jnp.bfloat16)

def norm_back(inputs, grad_rows, gain_row, grad_normed):
    widened = inputs.astype(jnp.float32)
    inverse = lax.rsqrt(lax.optimization_barrier(jnp.mean(widened * widened, axis=-1, keepdims=True)) + 1e-05)
    scaled = grad_normed * gain_row
    middle = lax.optimization_barrier(jnp.mean(widened * scaled, axis=-1, keepdims=True))
    result = grad_rows.astype(jnp.float32) + inverse * scaled - widened * inverse * inverse * inverse * middle
    return result.astype(jnp.bfloat16)

def split_heads(qkv_rows):
    length = qkv_rows.shape[0]
    kv_local = qkv_rows.shape[1] // ((GROUP + 2) * HD)
    blocks = qkv_rows.reshape(length, kv_local, GROUP + 2, HD).astype(jnp.float32)
    return (blocks[:, :, :GROUP], blocks[:, :, GROUP], blocks[:, :, GROUP + 1])

def attention_probs(queries, keys):
    length = queries.shape[0]
    factor = 1.0 / jnp.sqrt(jnp.float32(HD))
    scores = jnp.einsum('tkgd,ukd->kgtu', queries, keys) * factor
    rows_at = lax.broadcasted_iota(jnp.int32, (length, length), 0)
    cols_at = lax.broadcasted_iota(jnp.int32, (length, length), 1)
    scores = jnp.where(cols_at > rows_at, -1e+30, scores)
    return jax.nn.softmax(scores, axis=-1)

def attend(qkv_rows):
    length = qkv_rows.shape[0]
    queries, keys, values = split_heads(qkv_rows)
    probs = attention_probs(queries, keys)
    probs_low = probs.astype(jnp.bfloat16).astype(jnp.float32)
    heads = jnp.einsum('kgtu,ukd->tkgd', probs_low, values)
    return heads.reshape(length, -1).astype(jnp.bfloat16)

def attend_back(qkv_rows, grad_heads):
    length = qkv_rows.shape[0]
    queries, keys, values = split_heads(qkv_rows)
    probs = attention_probs(queries, keys)
    probs_low = probs.astype(jnp.bfloat16).astype(jnp.float32)
    kv_local = keys.shape[1]
    grad_blocks = grad_heads.astype(jnp.float32).reshape(length, kv_local, GROUP, HD)
    factor = 1.0 / jnp.sqrt(jnp.float32(HD))
    grad_values = jnp.einsum('kgtu,tkgd->ukd', probs_low, grad_blocks)
    grad_probs = jnp.einsum('tkgd,ukd->kgtu', grad_blocks, values)
    grad_scores = probs * (grad_probs - lax.optimization_barrier(jnp.sum(probs * grad_probs, axis=-1, keepdims=True)))
    grad_queries = jnp.einsum('kgtu,ukd->tkgd', grad_scores, keys) * factor
    grad_keys = jnp.einsum('kgtu,tkgd->ukd', grad_scores, queries) * factor
    joined = jnp.concatenate([grad_queries, grad_keys[:, :, None], grad_values[:, :, None]], axis=2)
    return joined.reshape(length, -1).astype(jnp.bfloat16)

def block_sum(partial_value):
    rounded = lax.optimization_barrier(partial_value.astype(jnp.bfloat16))
    return lax.optimization_barrier(jnp.sum(rounded.astype(jnp.float32), axis=0))

def reference(x_fwd, x_bwd, grad_out, saved_qkv, norm_gain, w_qkv, w_out):
    width_heads = HEADS * HD // N_TENSOR
    width_merged = KVH * (GROUP + 2) * HD // N_TENSOR

    def one_section(section_args):
        fwd_in, bwd_in, grad_in, qkv_saved, gain_row, weight_qkv, weight_out = section_args
        normed = normalize(fwd_in, gain_row).reshape(N_DP * TOK, D)
        qkv_now = jnp.dot(normed, weight_qkv, preferred_element_type=jnp.float32).astype(jnp.bfloat16)
        heads_out = jax.vmap(attend)(qkv_now.reshape(N_DP, TOK, -1))
        partial_value = jnp.einsum('rtg,tgd->trd', heads_out.reshape(N_DP * TOK, N_TENSOR, width_heads).astype(jnp.float32), weight_out.reshape(N_TENSOR, width_heads, D).astype(jnp.float32))
        mixed = block_sum(partial_value).reshape(N_DP, TOK, D)
        output = (fwd_in.astype(jnp.float32) + mixed).astype(jnp.bfloat16)
        grad_heads = jnp.dot(grad_in.reshape(N_DP * TOK, D), weight_out.T, preferred_element_type=jnp.float32).astype(jnp.bfloat16)
        grad_qkv = jax.vmap(attend_back)(qkv_saved, grad_heads.reshape(N_DP, TOK, -1))
        partial_in = jnp.einsum('rtc,dtc->trd', grad_qkv.reshape(N_DP * TOK, N_TENSOR, width_merged).astype(jnp.float32), weight_qkv.reshape(D, N_TENSOR, width_merged).astype(jnp.float32))
        grad_normed = block_sum(partial_in).reshape(N_DP, TOK, D)
        grad_input = norm_back(bwd_in, grad_in, gain_row, grad_normed)
        return (output, grad_input)
    outputs, grads = lax.map(one_section, (x_fwd, x_bwd, grad_out, saved_qkv, norm_gain, w_qkv, w_out))
    return (jnp.roll(outputs, 1, axis=0), jnp.roll(grads, -1, axis=0))
```

```python
import jax
import jax.numpy as jnp
from jax import lax
from jax.sharding import PartitionSpec as P

HD = 128
GROUP = 6


def shift_pairs(count, steps):
    return [(source, (source + steps) % count) for source in range(count)]


def partner_pairs(count, step):
    if count & (count - 1):
        raise ValueError("dp size")
    return [(source, source ^ step) for source in range(count)]


def partner_index(axis, step):
    return jnp.bitwise_xor(lax.axis_index(axis), step)


def cross_pairs(step, forward):
    pipes = lax.axis_size("pipe")
    count = lax.axis_size("dp")
    return [
        (p * count + d, ((p + forward) % pipes) * count + (d ^ step))
        for p in range(pipes)
        for d in range(count)
    ]


def over_dp(value, step):
    return lax.ppermute(value, "dp", partner_pairs(lax.axis_size("dp"), step))


def over_pipe(value, steps):
    return lax.ppermute(value, "pipe", shift_pairs(lax.axis_size("pipe"), steps))


def gather_rolled(value, axis):
    count = lax.axis_size("tensor")
    blocks = [value]
    for step in range(1, count):
        blocks.append(lax.ppermute(value, "tensor", shift_pairs(count, -step)))
    return jnp.concatenate(blocks, axis=axis)


def scatter_rolled(value, axis):
    count = lax.axis_size("tensor")
    rows = value.shape[axis] // count
    total = lax.slice_in_dim(value, 0, rows, axis=axis).astype(jnp.float32)
    for step in range(1, count):
        block = lax.slice_in_dim(value, step * rows, (step + 1) * rows, axis=axis)
        total = total + lax.ppermute(block, "tensor", shift_pairs(count, step)).astype(jnp.float32)
    return total


def gather_dp(value):
    count = lax.axis_size("dp")
    if count != 4:
        return [value] + [over_dp(value, step) for step in range(1, count)]
    far = over_dp(value, 2)
    near = over_dp(value, 1)
    return [value, near, far, over_dp(far, 1)]


def scatter_dp(terms):
    count = lax.axis_size("dp")
    if count != 4:
        total = terms[0].astype(jnp.float32)
        for step in range(1, count):
            total = total + over_dp(terms[step], step).astype(jnp.float32)
        return total
    relay = over_dp(terms[3], 1)
    joined = (terms[2].astype(jnp.float32) + relay.astype(jnp.float32)).astype(terms[2].dtype)
    far = over_dp(joined, 2)
    near = over_dp(terms[1], 1)
    return terms[0].astype(jnp.float32) + near.astype(jnp.float32) + far.astype(jnp.float32)


def normalize(inputs, gain_row):
    widened = inputs.astype(jnp.float32)
    inverse = lax.rsqrt(jnp.mean(widened * widened, axis=-1, keepdims=True) + 1e-05)
    return (widened * inverse * gain_row).astype(jnp.bfloat16)


def norm_back(inputs, grad_rows, gain_row, grad_normed):
    widened = inputs.astype(jnp.float32)
    inverse = lax.rsqrt(jnp.mean(widened * widened, axis=-1, keepdims=True) + 1e-05)
    scaled = grad_normed * gain_row
    middle = jnp.mean(widened * scaled, axis=-1, keepdims=True)
    result = (
        grad_rows.astype(jnp.float32)
        + inverse * scaled
        - widened * inverse * inverse * inverse * middle
    )
    return result.astype(jnp.bfloat16)


def split_heads(qkv_rows):
    length = qkv_rows.shape[0]
    kv_local = qkv_rows.shape[1] // ((GROUP + 2) * HD)
    blocks = qkv_rows.reshape(length, kv_local, GROUP + 2, HD)
    return (blocks[:, :, :GROUP], blocks[:, :, GROUP], blocks[:, :, GROUP + 1])


def attention_probs(queries, keys, start):
    length = queries.shape[0]
    factor = 1.0 / jnp.sqrt(jnp.float32(HD))
    scores = (
        jnp.einsum("tkgd,ukd->kgtu", queries, keys, preferred_element_type=jnp.float32) * factor
    )
    rows_at = lax.rem(lax.broadcasted_iota(jnp.int32, (length, length), 0) + start, length)
    cols_at = lax.rem(lax.broadcasted_iota(jnp.int32, (length, length), 1) + start, length)
    scores = jnp.where(cols_at > rows_at, -1e30, scores)
    return jax.nn.softmax(scores, axis=-1)


def attend(qkv_rows, start):
    length = qkv_rows.shape[0]
    queries, keys, values = split_heads(qkv_rows)
    probs_low = attention_probs(queries, keys, start).astype(jnp.bfloat16)
    heads = jnp.einsum("kgtu,ukd->tkgd", probs_low, values, preferred_element_type=jnp.float32)
    return heads.reshape(length, -1).astype(jnp.bfloat16)


def attend_back(qkv_rows, grad_heads, start):
    length = qkv_rows.shape[0]
    queries, keys, values = split_heads(qkv_rows)
    probs = attention_probs(queries, keys, start)
    probs_low = probs.astype(jnp.bfloat16)
    kv_local = keys.shape[1]
    grad_blocks = grad_heads.reshape(length, kv_local, GROUP, HD)
    factor = 1.0 / jnp.sqrt(jnp.float32(HD))
    grad_values = jnp.einsum(
        "kgtu,tkgd->ukd", probs_low, grad_blocks, preferred_element_type=jnp.float32
    )
    grad_probs = jnp.einsum(
        "tkgd,ukd->kgtu", grad_blocks, values, preferred_element_type=jnp.float32
    )
    grad_scores = probs * (grad_probs - jnp.sum(probs * grad_probs, axis=-1, keepdims=True))
    grad_queries = jnp.einsum("kgtu,ukd->tkgd", grad_scores, keys.astype(jnp.float32)) * factor
    grad_keys = jnp.einsum("kgtu,tkgd->ukd", grad_scores, queries.astype(jnp.float32)) * factor
    joined = jnp.concatenate([grad_queries, grad_keys[:, :, None], grad_values[:, :, None]], axis=2)
    return joined.reshape(length, -1).astype(jnp.bfloat16)


def contract_last(left, right):
    return lax.dot_general(
        left, right, (((1,), (1,)), ((), ())), preferred_element_type=jnp.float32
    )


def per_device(x_fwd, x_bwd, grad_out, saved_qkv, norm_gain, w_qkv, w_out):
    fwd_rows = x_fwd[0, 0]
    bwd_rows = x_bwd[0, 0]
    grad_rows = grad_out[0, 0]
    qkv_saved = saved_qkv[0, 0]
    gain_row = norm_gain
    weight_qkv = w_qkv[0]
    weight_out = w_out[0]
    length = qkv_saved.shape[0]
    rows, width = fwd_rows.shape
    replicas = lax.axis_size("dp")
    columns = weight_out.shape[1]
    start = lax.axis_index("tensor") * rows

    def grad_piece(step):
        at = partner_index("dp", step) * columns
        return lax.dynamic_slice_in_dim(grad_rows, at, columns, axis=1)

    pieces = [over_dp(grad_piece(step), step) for step in range(1, replicas)]
    pieces = jnp.stack([grad_piece(0)] + pieces, axis=0)

    fwd_prev = over_pipe(fwd_rows, 1)
    bwd_next = over_pipe(bwd_rows, -1)
    grad_next = over_pipe(grad_rows, -1)
    gain_next = over_pipe(gain_row, -1)

    normed_full = gather_rolled(normalize(fwd_rows, gain_row), 0)
    qkv_now = jnp.dot(normed_full, weight_qkv, preferred_element_type=jnp.float32).astype(
        jnp.bfloat16
    )
    heads_out = attend(qkv_now, start)

    grad_cols = gather_rolled(pieces, 1).reshape(replicas * length, columns)
    grad_terms = contract_last(grad_cols, weight_out).astype(jnp.bfloat16)
    grad_terms = grad_terms.reshape(replicas, length, -1)
    grad_heads = scatter_dp([grad_terms[k] for k in range(replicas)]).astype(jnp.bfloat16)

    heads_all = jnp.concatenate(gather_dp(heads_out), axis=0)
    projected = jnp.dot(heads_all, weight_out, preferred_element_type=jnp.float32)
    projected = projected.astype(jnp.bfloat16).reshape(replicas, length, columns)
    summed = scatter_rolled(projected, 1).astype(jnp.bfloat16)
    output = fwd_prev.astype(jnp.float32)
    for step in range(replicas):
        piece = lax.ppermute(summed[step], ("pipe", "dp"), cross_pairs(step, 1))
        at = partner_index("dp", step) * columns
        part = lax.dynamic_slice_in_dim(fwd_prev, at, columns, axis=1).astype(jnp.float32)
        part = part + piece.astype(jnp.float32)
        output = lax.dynamic_update_slice_in_dim(output, part, at, axis=1)
    output = output.astype(jnp.bfloat16)

    qkv_rolled = jnp.roll(qkv_saved, -start, axis=0)
    grad_qkv = attend_back(qkv_rolled, grad_heads, start)
    chunks = 2
    chunk = width // chunks
    arrived = []
    for index in range(chunks):
        block = weight_qkv[index * chunk : (index + 1) * chunk]
        partial_in = contract_last(grad_qkv, block).astype(jnp.bfloat16)
        grad_normed = scatter_rolled(partial_in, 0).astype(jnp.bfloat16)
        arrived.append(over_pipe(grad_normed, -1))
    grad_normed = jnp.concatenate(arrived, axis=1).astype(jnp.float32)
    grad_input = norm_back(bwd_next, grad_next, gain_next, grad_normed)
    return (output[None, None], grad_input[None, None])


def solution(mesh):
    return jax.shard_map(
        per_device,
        mesh=mesh,
        in_specs=(
            P("pipe", "dp", "tensor", None),
            P("pipe", "dp", "tensor", None),
            P("pipe", "dp", "tensor", None),
            P("pipe", "dp", None, "tensor"),
            P("pipe", None),
            P("pipe", None, "tensor"),
            P("pipe", "tensor", "dp"),
        ),
        out_specs=(P("pipe", "dp", "tensor", None), P("pipe", "dp", "tensor", None)),
        check_vma=False,
    )
```

```python
import math

import jax
import jax.numpy as jnp
from jax import lax
from jax.experimental import pallas as pl
from jax.experimental.pallas import tpu as pltpu
from jax.sharding import PartitionSpec as P

HD = 128
GROUP = 6
UNIT = (GROUP + 2) * HD


def shift_pairs(count, steps):
    return [(source, (source + steps) % count) for source in range(count)]


def partner_pairs(count, step):
    if count & (count - 1):
        raise ValueError("dp size")
    return [(source, source ^ step) for source in range(count)]


def partner_index(axis, step):
    return jnp.bitwise_xor(lax.axis_index(axis), step)


def cross_pairs(step, forward):
    pipes = lax.axis_size("pipe")
    count = lax.axis_size("dp")
    return [
        (p * count + d, ((p + forward) % pipes) * count + (d ^ step))
        for p in range(pipes)
        for d in range(count)
    ]


def over_dp(value, step):
    return lax.ppermute(value, "dp", partner_pairs(lax.axis_size("dp"), step))


def over_pipe(value, steps):
    return lax.ppermute(value, "pipe", shift_pairs(lax.axis_size("pipe"), steps))


def blocks_of_cores(value):
    count = lax.axis_size("tensor")
    return [value] + [
        lax.ppermute(value, "tensor", shift_pairs(count, -step)) for step in range(1, count)
    ]


def sum_over_cores(keep, sends):
    count = lax.axis_size("tensor")
    total = keep.astype(jnp.float32)
    for step in range(1, count):
        block = lax.ppermute(sends[step - 1], "tensor", shift_pairs(count, step))
        total = total + block.astype(jnp.float32)
    return total


def normalize(inputs, gain_row):
    widened = inputs.astype(jnp.float32)
    inverse = lax.rsqrt(jnp.mean(widened * widened, axis=-1, keepdims=True) + 1e-05)
    return (widened * inverse * gain_row).astype(jnp.bfloat16)


def norm_back(inputs, grad_rows, gain_row, grad_normed):
    widened = inputs.astype(jnp.float32)
    inverse = lax.rsqrt(jnp.mean(widened * widened, axis=-1, keepdims=True) + 1e-05)
    scaled = grad_normed * gain_row
    middle = jnp.mean(widened * scaled, axis=-1, keepdims=True)
    result = (
        grad_rows.astype(jnp.float32)
        + inverse * scaled
        - widened * inverse * inverse * inverse * middle
    )
    return result.astype(jnp.bfloat16)


def mxu(left, right, left_dim, right_dim):
    return lax.dot_general(
        left,
        right,
        (((left_dim,), (right_dim,)), ((), ())),
        preferred_element_type=jnp.float32,
    )


def later_keys(length, start):
    rows_at = lax.broadcasted_iota(jnp.int32, (length, length), 0) + start
    cols_at = lax.broadcasted_iota(jnp.int32, (length, length), 1) + start
    rows_at = jnp.where(rows_at >= length, rows_at - length, rows_at)
    cols_at = jnp.where(cols_at >= length, cols_at - length, cols_at)
    return cols_at > rows_at


def head_columns(value, head):
    return value[:, head * HD : (head + 1) * HD]


def stacked_heads(value):
    return jnp.concatenate([head_columns(value, g) for g in range(GROUP)], axis=0)


def probabilities(queries, keys, masked):
    length = keys.shape[0]
    scores = mxu(queries, keys, 1, 1) * (1.0 / math.sqrt(HD))
    rows = []
    for g in range(GROUP):
        part = jnp.where(masked, -1e30, scores[g * length : (g + 1) * length])
        part = jnp.exp(part - jnp.max(part, axis=-1, keepdims=True))
        rows.append(part / jnp.sum(part, axis=-1, keepdims=True))
    return jnp.concatenate(rows, axis=0)


def attend_unit(qkv, masked, out_ref):
    length = qkv.shape[0]
    keys, values = head_columns(qkv, GROUP), head_columns(qkv, GROUP + 1)
    probs = probabilities(stacked_heads(qkv), keys, masked).astype(jnp.bfloat16)
    heads = mxu(probs, values, 1, 0).astype(jnp.bfloat16)
    for g in range(GROUP):
        out_ref[:, g * HD : (g + 1) * HD] = heads[g * length : (g + 1) * length]


def attend_back_unit(qkv, grads, masked, out_ref, at):
    length = qkv.shape[0]
    factor = 1.0 / math.sqrt(HD)
    keys, values = head_columns(qkv, GROUP), head_columns(qkv, GROUP + 1)
    queries = stacked_heads(qkv)
    grads = stacked_heads(grads)
    probs = probabilities(queries, keys, masked)
    grad_values = mxu(probs.astype(jnp.bfloat16), grads, 0, 0)
    grad_probs = mxu(grads, values, 1, 1)
    grad_scores = probs * (grad_probs - jnp.sum(probs * grad_probs, axis=-1, keepdims=True))
    grad_scores = grad_scores.astype(jnp.bfloat16)
    grad_queries = mxu(grad_scores, keys, 1, 0) * factor
    grad_keys = mxu(grad_scores, queries, 0, 0) * factor
    for g in range(GROUP):
        out_ref[:, at + g * HD : at + (g + 1) * HD] = grad_queries[
            g * length : (g + 1) * length
        ].astype(jnp.bfloat16)
    out_ref[:, at + GROUP * HD : at + (GROUP + 1) * HD] = grad_keys.astype(jnp.bfloat16)
    out_ref[:, at + (GROUP + 1) * HD : at + UNIT] = grad_values.astype(jnp.bfloat16)


def divisor(size, most):
    parts = 1
    while size % parts or size // parts > most or (size // parts) % HD:
        parts += 1
        if parts > size:
            raise ValueError("block size")
    return size // parts


def resident(shape):
    zeros = (0,) * len(shape)
    return pl.BlockSpec(shape, lambda *_: zeros)


SCALAR = pl.BlockSpec(memory_space=pltpu.SMEM)


def params(mebibytes):
    return pltpu.CompilerParams(vmem_limit_bytes=mebibytes << 20)


def cost(flops, moved):
    return pl.CostEstimate(flops=flops, bytes_accessed=moved, transcendentals=0)


def forward_heads(batches, weight, start):
    rows, width = batches[0][0].shape
    cores = len(batches[0])
    length = rows * cores
    merged = weight.shape[1]
    units = merged // UNIT
    depth = divisor(width, 1024)
    total = length * len(batches)
    flat = [block for blocks in batches for block in blocks]

    def kernel(start_ref, *refs):
        ins, (weight_ref, *outs), total_ref = refs[: len(flat)], refs[len(flat) : -1], refs[-1]
        step = pl.program_id(1)
        at = pl.ds(pl.multiple_of(step * depth, depth), depth)
        left = jnp.concatenate([ref[:, at] for ref in ins], axis=0)
        product = jnp.dot(left, weight_ref[...], preferred_element_type=jnp.float32)

        @pl.when(step == 0)
        def _():
            total_ref[...] = product

        @pl.when(step > 0)
        def _():
            total_ref[...] += product

        @pl.when(step == pl.num_programs(1) - 1)
        def _():
            masked = later_keys(length, start_ref[0])
            for index, out_ref in enumerate(outs):
                qkv = total_ref[index * length : (index + 1) * length].astype(jnp.bfloat16)
                attend_unit(qkv, masked, out_ref)

    return pl.pallas_call(
        kernel,
        grid=(units, width // depth),
        in_specs=[SCALAR]
        + [resident((rows, width)) for _ in flat]
        + [pl.BlockSpec((depth, UNIT), lambda j, k: (k, j))],
        out_specs=[pl.BlockSpec((length, GROUP * HD), lambda j, k: (0, j)) for _ in batches],
        out_shape=[
            jax.ShapeDtypeStruct((length, units * GROUP * HD), jnp.bfloat16) for _ in batches
        ],
        scratch_shapes=[pltpu.VMEM((total, UNIT), jnp.float32)],
        compiler_params=params(32),
        cost_estimate=cost(2 * total * width * merged, 2 * width * merged),
        name="forward_heads",
    )(start, *flat, weight)


def head_terms(pieces, weight):
    rows, columns = pieces[0][0].shape
    cores = len(pieces[0])
    length = rows * cores
    depth = weight.shape[0]
    block = divisor(depth, 768)
    flat = [part for parts in pieces for part in parts]

    def kernel(*refs):
        ins, weight_ref, outs = refs[: len(flat)], refs[len(flat)], refs[len(flat) + 1 :]
        left = jnp.concatenate([ref[...] for ref in ins], axis=0)
        product = mxu(left, weight_ref[...], 1, 1).astype(jnp.bfloat16)
        for index, out_ref in enumerate(outs):
            out_ref[...] = product[index * length : (index + 1) * length]

    return pl.pallas_call(
        kernel,
        grid=(depth // block,),
        in_specs=[resident((rows, columns)) for _ in flat]
        + [pl.BlockSpec((block, columns), lambda j: (j, 0))],
        out_specs=[pl.BlockSpec((length, block), lambda j: (0, j)) for _ in pieces],
        out_shape=[jax.ShapeDtypeStruct((length, depth), jnp.bfloat16) for _ in pieces],
        compiler_params=params(24),
        cost_estimate=cost(2 * len(pieces) * length * depth * columns, 2 * depth * columns),
        name="head_terms",
    )(*flat, weight)


def project(heads, weight, cores):
    length, depth = heads[0].shape
    columns = weight.shape[1]
    rows = length // cores
    block = divisor(depth, 768)
    count = len(heads)

    def kernel(*refs):
        ins, weight_ref, outs, total_ref = refs[:count], refs[count], refs[count + 1 : -1], refs[-1]
        step = pl.program_id(0)
        left = jnp.concatenate([ref[...] for ref in ins], axis=0)
        product = jnp.dot(left, weight_ref[...], preferred_element_type=jnp.float32)

        @pl.when(step == 0)
        def _():
            total_ref[...] = product

        @pl.when(step > 0)
        def _():
            total_ref[...] += product

        @pl.when(step == pl.num_programs(0) - 1)
        def _():
            for core, out_ref in enumerate(outs):
                for index in range(count):
                    at = index * length + core * rows
                    out_ref[index * rows : (index + 1) * rows] = total_ref[at : at + rows].astype(
                        jnp.bfloat16
                    )

    return pl.pallas_call(
        kernel,
        grid=(depth // block,),
        in_specs=[pl.BlockSpec((length, block), lambda j: (0, j)) for _ in heads]
        + [pl.BlockSpec((block, columns), lambda j: (j, 0))],
        out_specs=[resident((count * rows, columns)) for _ in range(cores)],
        out_shape=[
            jax.ShapeDtypeStruct((count * rows, columns), jnp.bfloat16) for _ in range(cores)
        ],
        scratch_shapes=[pltpu.VMEM((count * length, columns), jnp.float32)],
        compiler_params=params(24),
        cost_estimate=cost(2 * count * length * depth * columns, 2 * depth * columns),
        name="project",
    )(*heads, weight)


def back_first(qkv, terms, weight, start, cores, steps, block):
    length, merged = qkv.shape
    units = merged // UNIT
    rows = length // cores

    def kernel(start_ref, qkv_ref, *refs):
        ins = refs[: len(terms)]
        weight_ref, grad_ref, *outs = refs[len(terms) :]

        @pl.when(pl.program_id(0) == 0)
        def _():
            masked = later_keys(length, start_ref[0])
            for unit in range(units):
                at = unit * UNIT
                part = slice(unit * GROUP * HD, (unit + 1) * GROUP * HD)
                grads = ins[0][:, part].astype(jnp.float32)
                for ref in ins[1:]:
                    grads = grads + ref[:, part].astype(jnp.float32)
                attend_back_unit(
                    qkv_ref[:, at : at + UNIT], grads.astype(jnp.bfloat16), masked, grad_ref, at
                )

        product = mxu(grad_ref[...], weight_ref[...], 1, 1).astype(jnp.bfloat16)
        for core, out_ref in enumerate(outs):
            out_ref[...] = product[core * rows : (core + 1) * rows]

    results = pl.pallas_call(
        kernel,
        grid=(steps,),
        in_specs=[SCALAR, resident(qkv.shape)]
        + [resident(term.shape) for term in terms]
        + [pl.BlockSpec((block, merged), lambda j: (j, 0))],
        out_specs=[resident(qkv.shape)]
        + [pl.BlockSpec((rows, block), lambda j: (0, j)) for _ in range(cores)],
        out_shape=[jax.ShapeDtypeStruct(qkv.shape, jnp.bfloat16)]
        + [jax.ShapeDtypeStruct((rows, steps * block), jnp.bfloat16) for _ in range(cores)],
        compiler_params=params(32),
        cost_estimate=cost(2 * length * merged * steps * block, 2 * merged * steps * block),
        name="back_first",
    )(start, qkv, *terms, weight)
    return results[0], results[1:]


def back_rest(grad_qkv, weight, cores, first, steps, block):
    length, merged = grad_qkv.shape
    rows = length // cores

    def kernel(grad_ref, weight_ref, *outs):
        product = mxu(grad_ref[...], weight_ref[...], 1, 1).astype(jnp.bfloat16)
        for core, out_ref in enumerate(outs):
            out_ref[...] = product[core * rows : (core + 1) * rows]

    return pl.pallas_call(
        kernel,
        grid=(steps,),
        in_specs=[
            resident(grad_qkv.shape),
            pl.BlockSpec((block, merged), lambda j: (first + j, 0)),
        ],
        out_specs=[pl.BlockSpec((rows, block), lambda j: (0, j)) for _ in range(cores)],
        out_shape=[
            jax.ShapeDtypeStruct((rows, steps * block), jnp.bfloat16) for _ in range(cores)
        ],
        compiler_params=params(32),
        cost_estimate=cost(2 * length * merged * steps * block, 2 * merged * steps * block),
        name="back_rest",
    )(grad_qkv, weight)


def scatter_dp(terms):
    if len(terms) != 4:
        return [terms[0]] + [over_dp(terms[step], step) for step in range(1, len(terms))]
    relay = over_dp(terms[3], 1)
    near = over_dp(terms[1], 1)
    joined = (terms[2].astype(jnp.float32) + relay.astype(jnp.float32)).astype(jnp.bfloat16)
    return [terms[0], near, over_dp(joined, 2)]


def per_device(x_fwd, x_bwd, grad_out, saved_qkv, norm_gain, w_qkv, w_out):
    fwd_rows = x_fwd[0, 0]
    bwd_rows = x_bwd[0, 0]
    grad_rows = grad_out[0, 0]
    qkv_saved = saved_qkv[0, 0]
    gain_row = norm_gain
    weight_qkv = w_qkv[0]
    weight_out = w_out[0]
    rows, width = fwd_rows.shape
    cores = lax.axis_size("tensor")
    replicas = lax.axis_size("dp")
    columns = weight_out.shape[1]
    start = lax.axis_index("tensor") * rows
    start_word = jnp.full((1,), start, jnp.int32)

    def grad_piece(step):
        at = partner_index("dp", step) * columns
        return lax.dynamic_slice_in_dim(grad_rows, at, columns, axis=1)

    pieces = [grad_piece(0)] + [over_dp(grad_piece(step), step) for step in range(1, replicas)]

    normed_rows = normalize(fwd_rows, gain_row)
    batches = [blocks_of_cores(normed_rows)]
    if replicas == 4:
        batches.append(blocks_of_cores(over_dp(normed_rows, 1)))

    terms = head_terms([blocks_of_cores(piece) for piece in pieces], weight_out)
    batches, terms = lax.optimization_barrier((batches, terms))
    terms = scatter_dp(terms)

    heads = forward_heads(batches, weight_qkv, start_word)
    if replicas == 4:
        far = over_dp(heads[0], 2)
        heads = [heads[0], heads[1], far, over_dp(far, 1)]
        groups = [(0, 1, 2), (3,)]
    else:
        heads = heads + [over_dp(heads[0], step) for step in range(1, replicas)]
        groups = [tuple(range(replicas))]

    fwd_prev = over_pipe(fwd_rows, 1)
    bwd_next = over_pipe(bwd_rows, -1)
    grad_next = over_pipe(grad_rows, -1)
    gain_next = over_pipe(gain_row, -1)

    qkv_rolled = jnp.roll(qkv_saved, -start, axis=0)
    block = divisor(width // 2, 512)
    steps = width // 2 // block
    grad_qkv, (keep, *sends) = back_first(
        qkv_rolled, terms, weight_qkv, start_word, cores, steps, block
    )
    arrived = [over_pipe(sum_over_cores(keep, sends).astype(jnp.bfloat16), -1)]
    keep, *sends = back_rest(grad_qkv, weight_qkv, cores, steps, steps, block)
    arrived.append(over_pipe(sum_over_cores(keep, sends).astype(jnp.bfloat16), -1))
    grad_normed = jnp.concatenate(arrived, axis=1).astype(jnp.float32)
    grad_input = norm_back(bwd_next, grad_next, gain_next, grad_normed)

    output = fwd_prev
    for group in groups:
        keep, *sends = project([heads[step] for step in group], weight_out, cores)
        summed = sum_over_cores(keep, sends).astype(jnp.bfloat16)
        for index, step in enumerate(group):
            piece = lax.ppermute(
                summed[index * rows : (index + 1) * rows], ("pipe", "dp"), cross_pairs(step, 1)
            )
            at = partner_index("dp", step) * columns
            part = lax.dynamic_slice_in_dim(fwd_prev, at, columns, axis=1).astype(jnp.float32)
            part = (part + piece.astype(jnp.float32)).astype(jnp.bfloat16)
            output = lax.dynamic_update_slice_in_dim(output, part, at, axis=1)
    return (output[None, None], grad_input[None, None])


def solution(mesh):
    return jax.shard_map(
        per_device,
        mesh=mesh,
        in_specs=(
            P("pipe", "dp", "tensor", None),
            P("pipe", "dp", "tensor", None),
            P("pipe", "dp", "tensor", None),
            P("pipe", "dp", None, "tensor"),
            P("pipe", None),
            P("pipe", None, "tensor"),
            P("pipe", "tensor", "dp"),
        ),
        out_specs=(P("pipe", "dp", "tensor", None), P("pipe", "dp", "tensor", None)),
        check_vma=False,
    )
```

```python
import math

import jax
import jax.numpy as jnp
from jax import lax
from jax.experimental import pallas as pl
from jax.experimental.pallas import tpu as pltpu
from jax.sharding import PartitionSpec as P


HD = 128
GROUP = 6
UNIT = (GROUP + 2) * HD


def shift_pairs(count, steps):
    return [(source, (source + steps) % count) for source in range(count)]


def partner_pairs(count, step):
    if count & (count - 1):
        raise ValueError("dp size")
    return [(source, source ^ step) for source in range(count)]


def partner_index(axis, step):
    return jnp.bitwise_xor(lax.axis_index(axis), step)


def cross_pairs(step, forward):
    pipes = lax.axis_size("pipe")
    count = lax.axis_size("dp")
    return [
        (p * count + d, ((p + forward) % pipes) * count + (d ^ step))
        for p in range(pipes)
        for d in range(count)
    ]


def over_dp(value, step):
    return lax.ppermute(value, "dp", partner_pairs(lax.axis_size("dp"), step))


def over_pipe(value, steps):
    return lax.ppermute(value, "pipe", shift_pairs(lax.axis_size("pipe"), steps))


def blocks_of_cores(value):
    count = lax.axis_size("tensor")
    return [value] + [
        lax.ppermute(value, "tensor", shift_pairs(count, -step)) for step in range(1, count)
    ]


def sum_over_cores(keep, sends):
    count = lax.axis_size("tensor")
    total = keep.astype(jnp.float32)
    for step in range(1, count):
        block = lax.ppermute(sends[step - 1], "tensor", shift_pairs(count, step))
        total = total + block.astype(jnp.float32)
    return total


def normalize(inputs, gain_row):
    widened = inputs.astype(jnp.float32)
    inverse = lax.rsqrt(jnp.mean(widened * widened, axis=-1, keepdims=True) + 1e-05)
    return (widened * inverse * gain_row).astype(jnp.bfloat16)


def norm_back(inputs, grad_rows, scaled):
    widened = inputs.astype(jnp.float32)
    inverse = lax.rsqrt(jnp.mean(widened * widened, axis=-1, keepdims=True) + 1e-05)
    middle = jnp.mean(widened * scaled, axis=-1, keepdims=True)
    result = (
        grad_rows.astype(jnp.float32)
        + inverse * scaled
        - widened * inverse * inverse * inverse * middle
    )
    return result.astype(jnp.bfloat16)


def mxu(left, right, left_dim, right_dim):
    return lax.dot_general(
        left,
        right,
        (((left_dim,), (right_dim,)), ((), ())),
        preferred_element_type=jnp.float32,
    )


def later_keys(length, start):
    rows_at = lax.broadcasted_iota(jnp.int32, (length, length), 0) + start
    cols_at = lax.broadcasted_iota(jnp.int32, (length, length), 1) + start
    rows_at = jnp.where(rows_at >= length, rows_at - length, rows_at)
    cols_at = jnp.where(cols_at >= length, cols_at - length, cols_at)
    return cols_at > rows_at


def head_columns(value, head):
    return value[:, head * HD : (head + 1) * HD]


def stacked_heads(value):
    return jnp.concatenate([head_columns(value, g) for g in range(GROUP)], axis=0)


def probabilities(queries, keys, masked):
    length = keys.shape[0]
    scores = mxu(queries, keys, 1, 1) * (1.0 / math.sqrt(HD))
    rows = []
    for g in range(GROUP):
        part = jnp.where(masked, -1e30, scores[g * length : (g + 1) * length])
        part = jnp.exp(part - jnp.max(part, axis=-1, keepdims=True))
        rows.append(part / jnp.sum(part, axis=-1, keepdims=True))
    return jnp.concatenate(rows, axis=0)


def attend_unit(qkv, masked, out_ref, at):
    length = qkv.shape[0]
    keys, values = head_columns(qkv, GROUP), head_columns(qkv, GROUP + 1)
    probs = probabilities(stacked_heads(qkv), keys, masked).astype(jnp.bfloat16)
    heads = mxu(probs, values, 1, 0).astype(jnp.bfloat16)
    for g in range(GROUP):
        out_ref[:, at + g * HD : at + (g + 1) * HD] = heads[g * length : (g + 1) * length]


def attend_back_unit(qkv, grads, masked, out_ref, at):
    length = qkv.shape[0]
    factor = 1.0 / math.sqrt(HD)
    keys, values = head_columns(qkv, GROUP), head_columns(qkv, GROUP + 1)
    queries = stacked_heads(qkv)
    grads = stacked_heads(grads)
    probs = probabilities(queries, keys, masked)
    grad_values = mxu(probs.astype(jnp.bfloat16), grads, 0, 0)
    grad_probs = mxu(grads, values, 1, 1)
    grad_scores = probs * (grad_probs - jnp.sum(probs * grad_probs, axis=-1, keepdims=True))
    grad_scores = grad_scores.astype(jnp.bfloat16)
    grad_queries = mxu(grad_scores, keys, 1, 0) * factor
    grad_keys = mxu(grad_scores, queries, 0, 0) * factor
    for g in range(GROUP):
        out_ref[:, at + g * HD : at + (g + 1) * HD] = grad_queries[
            g * length : (g + 1) * length
        ].astype(jnp.bfloat16)
    out_ref[:, at + GROUP * HD : at + (GROUP + 1) * HD] = grad_keys.astype(jnp.bfloat16)
    out_ref[:, at + (GROUP + 1) * HD : at + UNIT] = grad_values.astype(jnp.bfloat16)


def divisor(size, most):
    parts = 1
    while size % parts or size // parts > most or (size // parts) % HD:
        parts += 1
        if parts > size:
            raise ValueError("block size")
    return size // parts


SCALAR = pl.BlockSpec(memory_space=pltpu.SMEM)
LOCAL = pl.BlockSpec(memory_space=pltpu.VMEM)
REMOTE = pl.BlockSpec(memory_space=pltpu.HBM)


def call(kernel, args, weight, outs, copies, block, scratch, flops):
    count = len(args)

    def body(*refs):
        ins, weight_ref = refs[:count], refs[count]
        results = refs[count + 1 : count + 1 + len(outs)]
        held, sems, *rest = refs[count + 1 + len(outs) :]
        moves = [
            pltpu.make_async_copy(
                weight_ref.at[pl.ds(row, block[0]), pl.ds(column, block[1])],
                held.at[index],
                sems.at[index],
            )
            for index, (row, column) in enumerate(copies)
        ]
        for move in moves:
            move.start()
        kernel(ins, results, held, lambda index: moves[index].wait(), *rest)

    moved = 2 * len(copies) * block[0] * block[1]
    return pl.pallas_call(
        body,
        in_specs=[SCALAR if arg.dtype == jnp.int32 else LOCAL for arg in args] + [REMOTE],
        out_specs=[LOCAL for _ in outs],
        out_shape=[jax.ShapeDtypeStruct(shape, jnp.bfloat16) for shape in outs],
        scratch_shapes=[
            pltpu.VMEM((len(copies),) + block, jnp.bfloat16),
            pltpu.SemaphoreType.DMA((len(copies),)),
        ]
        + scratch,
        compiler_params=pltpu.CompilerParams(vmem_limit_bytes=moved + (8 << 20)),
        cost_estimate=pl.CostEstimate(flops=flops, bytes_accessed=moved, transcendentals=0),
    )(*args, weight)


def forward_heads(blocks, weight, start):
    rows, width = blocks[0].shape
    length = rows * len(blocks)
    merged = weight.shape[1]
    units = merged // UNIT
    depth = divisor(width, 1024)
    steps = width // depth

    def kernel(ins, outs, held, wait):
        masked = later_keys(length, ins[0][0])
        for unit in range(units):
            total = None
            for step in range(steps):
                at = slice(step * depth, (step + 1) * depth)
                left = jnp.concatenate([ref[:, at] for ref in ins[1:]], axis=0)
                wait(unit * steps + step)
                product = mxu(left, held[unit * steps + step], 1, 0)
                total = product if total is None else total + product
            attend_unit(total.astype(jnp.bfloat16), masked, outs[0], unit * GROUP * HD)

    copies = [(step * depth, unit * UNIT) for unit in range(units) for step in range(steps)]
    return call(
        kernel,
        [start] + blocks,
        weight,
        [(length, units * GROUP * HD)],
        copies,
        (depth, UNIT),
        [],
        2 * length * width * merged,
    )[0]


def head_terms(pieces, weight):
    rows, columns = pieces[0][0].shape
    length = rows * len(pieces[0])
    depth = weight.shape[0]
    block = divisor(depth, 768)
    flat = [part for parts in pieces for part in parts]

    def kernel(ins, outs, held, wait):
        left = jnp.concatenate([ref[...] for ref in ins], axis=0)
        for step in range(depth // block):
            wait(step)
            product = mxu(left, held[step], 1, 1).astype(jnp.bfloat16)
            for index, out_ref in enumerate(outs):
                out_ref[:, step * block : (step + 1) * block] = product[
                    index * length : (index + 1) * length
                ]

    return call(
        kernel,
        flat,
        weight,
        [(length, depth) for _ in pieces],
        [(row, 0) for row in range(0, depth, block)],
        (block, columns),
        [],
        2 * len(pieces) * length * depth * columns,
    )


def project(heads, weight, cores):
    length, depth = heads[0].shape
    columns = weight.shape[1]
    rows = length // cores
    block = divisor(depth, 768)
    count = len(heads)

    def kernel(ins, outs, held, wait):
        total = None
        for step in range(depth // block):
            at = slice(step * block, (step + 1) * block)
            left = jnp.concatenate([ref[:, at] for ref in ins], axis=0)
            wait(step)
            product = mxu(left, held[step], 1, 0)
            total = product if total is None else total + product
        total = total.astype(jnp.bfloat16)
        for core, out_ref in enumerate(outs):
            for index in range(count):
                at = index * length + core * rows
                out_ref[index * rows : (index + 1) * rows] = total[at : at + rows]

    return call(
        kernel,
        heads,
        weight,
        [(count * rows, columns) for _ in range(cores)],
        [(row, 0) for row in range(0, depth, block)],
        (block, columns),
        [],
        2 * count * length * depth * columns,
    )


def back_columns(grad, outs, held, wait, cores, steps, block):
    rows = grad.shape[0] // cores
    for step in range(steps):
        wait(step)
        product = mxu(grad, held[step], 1, 1).astype(jnp.bfloat16)
        for core, out_ref in enumerate(outs):
            out_ref[:, step * block : (step + 1) * block] = product[
                core * rows : (core + 1) * rows
            ]


def back_first(qkv, terms, weight, start, cores, steps, block):
    length, merged = qkv.shape
    units = merged // UNIT
    rows = length // cores

    def kernel(ins, outs, held, wait):
        masked = later_keys(length, ins[0][0])
        for unit in range(units):
            at = unit * UNIT
            part = slice(unit * GROUP * HD, (unit + 1) * GROUP * HD)
            grads = ins[2][:, part].astype(jnp.float32)
            for ref in ins[3:]:
                grads = grads + ref[:, part].astype(jnp.float32)
            attend_back_unit(
                ins[1][:, at : at + UNIT], grads.astype(jnp.bfloat16), masked, outs[0], at
            )
        back_columns(outs[0][...], outs[1:], held, wait, cores, steps, block)

    results = call(
        kernel,
        [start, qkv] + terms,
        weight,
        [qkv.shape] + [(rows, steps * block) for _ in range(cores)],
        [(step * block, 0) for step in range(steps)],
        (block, merged),
        [],
        2 * length * merged * steps * block,
    )
    return results[0], results[1:]


def back_rest(grad_qkv, weight, cores, first, steps, block):
    length, merged = grad_qkv.shape
    rows = length // cores

    def kernel(ins, outs, held, wait):
        back_columns(ins[0][...], outs, held, wait, cores, steps, block)

    return call(
        kernel,
        [grad_qkv],
        weight,
        [(rows, steps * block) for _ in range(cores)],
        [((first + step) * block, 0) for step in range(steps)],
        (block, merged),
        [],
        2 * length * merged * steps * block,
    )


def per_device(x_fwd, x_bwd, grad_out, saved_qkv, norm_gain, w_qkv, w_out):
    return window(
        x_fwd[0, 0],
        x_bwd[0, 0],
        grad_out[0, 0],
        saved_qkv[0, 0],
        norm_gain,
        w_qkv[0],
        w_out[0],
    )


def window(fwd_rows, bwd_rows, grad_rows, qkv_saved, gain_row, weight_qkv, weight_out):
    rows, width = fwd_rows.shape
    cores = lax.axis_size("tensor")
    replicas = lax.axis_size("dp")
    columns = weight_out.shape[1]
    start = lax.axis_index("tensor") * rows
    start_word = jnp.full((1,), start, jnp.int32)
    if replicas != 4:
        raise ValueError("dp size")

    def grad_piece(step):
        at = partner_index("dp", step) * columns
        return lax.dynamic_slice_in_dim(grad_rows, at, columns, axis=1)

    pieces = [grad_piece(0)]
    pieces += [over_dp(grad_piece(step), step) for step in range(1, replicas)]

    normed_rows = normalize(fwd_rows, gain_row)
    normed_far = over_dp(normed_rows, 2)
    own_heads = forward_heads(blocks_of_cores(normed_rows), weight_qkv, start_word)
    far_heads = forward_heads(blocks_of_cores(normed_far), weight_qkv, start_word)
    near_heads = over_dp(own_heads, 1)
    last_heads = over_dp(far_heads, 1)

    exchanged = [blocks_of_cores(piece) for piece in pieces]
    terms = head_terms(exchanged, weight_out)
    relay = over_dp(terms[3], 1)
    near = over_dp(terms[1], 1)
    joined = (terms[2].astype(jnp.float32) + relay.astype(jnp.float32)).astype(jnp.bfloat16)
    terms = [terms[0], near, over_dp(joined, 2)]

    fwd_prev = over_pipe(fwd_rows, 1)
    bwd_next = over_pipe(bwd_rows, -1)
    grad_next = over_pipe(grad_rows, -1)

    qkv_rolled = jnp.roll(qkv_saved, -start, axis=0)
    half = width // 2
    block = divisor(half, 512)
    steps = half // block
    grad_qkv, (keep, *sends) = back_first(
        qkv_rolled, terms, weight_qkv, start_word, cores, steps, block
    )
    scaled = sum_over_cores(keep, sends) * gain_row[:, :half]
    arrived = [over_pipe(scaled.astype(jnp.bfloat16), -1)]
    keep, *sends = back_rest(grad_qkv, weight_qkv, cores, steps, steps, block)
    scaled = sum_over_cores(keep, sends) * gain_row[:, half:]
    arrived.append(over_pipe(scaled.astype(jnp.bfloat16), -1))
    scaled = jnp.concatenate(arrived, axis=1).astype(jnp.float32)
    grad_input = norm_back(bwd_next, grad_next, scaled)

    output = fwd_prev
    groups = (((0, 2), [own_heads, far_heads]), ((1, 3), [near_heads, last_heads]))
    for group, heads in groups:
        keep, *sends = project(heads, weight_out, cores)
        summed = sum_over_cores(keep, sends).astype(jnp.bfloat16)
        for index, step in enumerate(group):
            piece = lax.ppermute(
                summed[index * rows : (index + 1) * rows],
                ("pipe", "dp"),
                cross_pairs(step, 1),
            )
            at = partner_index("dp", step) * columns
            part = lax.dynamic_slice_in_dim(fwd_prev, at, columns, axis=1).astype(jnp.float32)
            part = (part + piece.astype(jnp.float32)).astype(jnp.bfloat16)
            output = lax.dynamic_update_slice_in_dim(output, part, at, axis=1)
    return (output[None, None], grad_input[None, None])


def solution(mesh):
    return jax.shard_map(
        per_device,
        mesh=mesh,
        in_specs=(
            P("pipe", "dp", "tensor", None),
            P("pipe", "dp", "tensor", None),
            P("pipe", "dp", "tensor", None),
            P("pipe", "dp", None, "tensor"),
            P("pipe", None),
            P("pipe", None, "tensor"),
            P("pipe", "tensor", "dp"),
        ),
        out_specs=(P("pipe", "dp", "tensor", None), P("pipe", "dp", "tensor", None)),
        check_vma=False,
    )
```

```python
import math

import jax
import jax.numpy as jnp
from jax import lax
from jax.experimental import pallas as pl
from jax.experimental.pallas import tpu as pltpu
from jax.sharding import PartitionSpec as P


HD = 128
GROUP = 6
UNIT = (GROUP + 2) * HD


def shift_pairs(count, steps):
    return [(source, (source + steps) % count) for source in range(count)]


def partner_pairs(count, step):
    if count & (count - 1):
        raise ValueError("dp size")
    return [(source, source ^ step) for source in range(count)]


def cross_pairs(step, forward):
    pipes = lax.axis_size("pipe")
    count = lax.axis_size("dp")
    return [
        (p * count + d, ((p + forward) % pipes) * count + (d ^ step))
        for p in range(pipes)
        for d in range(count)
    ]


def over_dp(value, step):
    return lax.ppermute(value, "dp", partner_pairs(lax.axis_size("dp"), step))


def over_pipe(value, steps):
    return lax.ppermute(value, "pipe", shift_pairs(lax.axis_size("pipe"), steps))


def blocks_of_cores(value):
    count = lax.axis_size("tensor")
    return [value] + [
        lax.ppermute(value, "tensor", shift_pairs(count, -step)) for step in range(1, count)
    ]


def sum_over_cores(keep, sends):
    count = lax.axis_size("tensor")
    total = keep.astype(jnp.float32)
    for step in range(1, count):
        block = lax.ppermute(sends[step - 1], "tensor", shift_pairs(count, step))
        total = total + block.astype(jnp.float32)
    return total


def normalize(inputs, gain_row):
    widened = inputs.astype(jnp.float32)
    inverse = lax.rsqrt(jnp.mean(widened * widened, axis=-1, keepdims=True) + 1e-05)
    return (widened * inverse * gain_row).astype(jnp.bfloat16)


def norm_back(inputs, grad_rows, scaled):
    widened = inputs.astype(jnp.float32)
    inverse = lax.rsqrt(jnp.mean(widened * widened, axis=-1, keepdims=True) + 1e-05)
    middle = jnp.mean(widened * scaled, axis=-1, keepdims=True)
    result = (
        grad_rows.astype(jnp.float32)
        + inverse * scaled
        - widened * inverse * inverse * inverse * middle
    )
    return result.astype(jnp.bfloat16)


def mxu(left, right, left_dim, right_dim):
    return lax.dot_general(
        left,
        right,
        (((left_dim,), (right_dim,)), ((), ())),
        preferred_element_type=jnp.float32,
    )


def later_keys(length, start):
    rows_at = lax.broadcasted_iota(jnp.int32, (length, length), 0) + start
    cols_at = lax.broadcasted_iota(jnp.int32, (length, length), 1) + start
    rows_at = jnp.where(rows_at >= length, rows_at - length, rows_at)
    cols_at = jnp.where(cols_at >= length, cols_at - length, cols_at)
    return cols_at > rows_at


def head_columns(value, head):
    return value[:, head * HD : (head + 1) * HD]


def stacked_heads(value):
    return jnp.concatenate([head_columns(value, g) for g in range(GROUP)], axis=0)


def probabilities(queries, keys, masked):
    length = keys.shape[0]
    scores = mxu(queries, keys, 1, 1) * (1.0 / math.sqrt(HD))
    rows = []
    for g in range(GROUP):
        part = jnp.where(masked, -1e30, scores[g * length : (g + 1) * length])
        part = jnp.exp(part - jnp.max(part, axis=-1, keepdims=True))
        rows.append(part / jnp.sum(part, axis=-1, keepdims=True))
    return jnp.concatenate(rows, axis=0)


def attend_unit(qkv, masked, out_ref, at):
    length = qkv.shape[0]
    keys, values = head_columns(qkv, GROUP), head_columns(qkv, GROUP + 1)
    probs = probabilities(stacked_heads(qkv), keys, masked).astype(jnp.bfloat16)
    heads = mxu(probs, values, 1, 0).astype(jnp.bfloat16)
    for g in range(GROUP):
        out_ref[:, at + g * HD : at + (g + 1) * HD] = heads[g * length : (g + 1) * length]


def attend_back_unit(qkv, grads, masked, out_ref, at):
    length = qkv.shape[0]
    factor = 1.0 / math.sqrt(HD)
    keys, values = head_columns(qkv, GROUP), head_columns(qkv, GROUP + 1)
    queries = stacked_heads(qkv)
    grads = stacked_heads(grads)
    probs = probabilities(queries, keys, masked)
    grad_values = mxu(probs.astype(jnp.bfloat16), grads, 0, 0)
    grad_probs = mxu(grads, values, 1, 1)
    grad_scores = probs * (grad_probs - jnp.sum(probs * grad_probs, axis=-1, keepdims=True))
    grad_scores = grad_scores.astype(jnp.bfloat16)
    grad_queries = mxu(grad_scores, keys, 1, 0) * factor
    grad_keys = mxu(grad_scores, queries, 0, 0) * factor
    for g in range(GROUP):
        out_ref[:, at + g * HD : at + (g + 1) * HD] = grad_queries[
            g * length : (g + 1) * length
        ].astype(jnp.bfloat16)
    out_ref[:, at + GROUP * HD : at + (GROUP + 1) * HD] = grad_keys.astype(jnp.bfloat16)
    out_ref[:, at + (GROUP + 1) * HD : at + UNIT] = grad_values.astype(jnp.bfloat16)


def divisor(size, most):
    parts = 1
    while size % parts or size // parts > most or (size // parts) % HD:
        parts += 1
        if parts > size:
            raise ValueError("block size")
    return size // parts


SCALAR = pl.BlockSpec(memory_space=pltpu.SMEM)
LOCAL = pl.BlockSpec(memory_space=pltpu.VMEM)
REMOTE = pl.BlockSpec(memory_space=pltpu.HBM)


def call(kernel, args, weight, outs, blocks, keep, flops):
    count = len(args)
    moved = 0
    if blocks:
        shape = (len(blocks), blocks[0][0].size, blocks[0][1].size)
        moved = 2 * math.prod(shape)

    def body(*refs):
        ins, weight_ref = refs[:count], refs[count]
        results = refs[count + 1 : count + 1 + len(outs)]
        if not blocks:
            kernel(ins, results, weight_ref, lambda index: None)
            return
        held, sems = refs[count + 1 + len(outs) :]
        moves = [
            pltpu.make_async_copy(weight_ref.at[part], held.at[index], sems.at[index])
            for index, part in enumerate(blocks)
        ]
        for move in moves:
            move.start()
        kernel(ins, results, held, lambda index: moves[index].wait())

    out_specs = [LOCAL for _ in outs]
    out_shape = [jax.ShapeDtypeStruct(out, jnp.bfloat16) for out in outs]
    scratch = []
    if blocks:
        scratch = [pltpu.SemaphoreType.DMA((len(blocks),))]
        if keep:
            out_specs.append(LOCAL)
            out_shape.append(pltpu.VMEM(shape, jnp.bfloat16))
        else:
            scratch.insert(0, pltpu.VMEM(shape, jnp.bfloat16))
        weight = pltpu.with_memory_space_constraint(weight, pltpu.HBM)
    else:
        weight = pltpu.with_memory_space_constraint(weight, pltpu.VMEM)
    limit = (0 if keep else moved) + (8 << 20)
    return pl.pallas_call(
        body,
        in_specs=[SCALAR if arg.dtype == jnp.int32 else LOCAL for arg in args]
        + [REMOTE if blocks else LOCAL],
        out_specs=out_specs,
        out_shape=out_shape,
        scratch_shapes=scratch,
        compiler_params=pltpu.CompilerParams(vmem_limit_bytes=limit),
        cost_estimate=pl.CostEstimate(flops=flops, bytes_accessed=moved, transcendentals=0),
    )(*args, weight)


def row_blocks(size, columns, most):
    block = divisor(size, most)
    return [(pl.ds(row, block), pl.ds(0, columns)) for row in range(0, size, block)]


def forward_heads(parts, weight, held, start):
    rows, width = parts[0].shape
    length = rows * len(parts)
    units = weight.shape[1] // UNIT
    depth = divisor(width, 1024)
    steps = width // depth

    def kernel(ins, outs, blocks, wait):
        masked = later_keys(length, ins[0][0])
        for unit in range(units):
            total = None
            for step in range(steps):
                at = slice(step * depth, (step + 1) * depth)
                left = jnp.concatenate([ref[:, at] for ref in ins[1:]], axis=0)
                wait(unit * steps + step)
                product = mxu(left, blocks[unit * steps + step], 1, 0)
                total = product if total is None else total + product
            attend_unit(total.astype(jnp.bfloat16), masked, outs[0], unit * GROUP * HD)

    blocks = [
        (pl.ds(step * depth, depth), pl.ds(unit * UNIT, UNIT))
        for unit in range(units)
        for step in range(steps)
    ]
    flops = 2 * length * width * units * UNIT
    outs = [(length, units * GROUP * HD)]
    if held is None:
        return call(kernel, [start] + parts, weight, outs, blocks, True, flops)
    return call(kernel, [start] + parts, held, outs, [], False, flops)[0]


def head_terms(pieces, weight):
    rows, columns = pieces[0][0].shape
    length = rows * len(pieces[0])
    depth = weight.shape[0]
    flat = [part for parts in pieces for part in parts]
    blocks = row_blocks(depth, columns, 768)
    block = depth // len(blocks)

    def kernel(ins, outs, held, wait):
        left = jnp.concatenate([ref[...] for ref in ins], axis=0)
        for step in range(len(blocks)):
            wait(step)
            product = mxu(left, held[step], 1, 1).astype(jnp.bfloat16)
            for index, out_ref in enumerate(outs):
                out_ref[:, step * block : (step + 1) * block] = product[
                    index * length : (index + 1) * length
                ]

    outs = [(length, depth) for _ in pieces]
    flops = 2 * len(pieces) * length * depth * columns
    *terms, held = call(kernel, flat, weight, outs, blocks, True, flops)
    return terms, held


def project(heads, held, cores):
    length, depth = heads[0].shape
    count, (steps, block, columns) = len(heads), held.shape
    rows = length // cores

    def kernel(ins, outs, blocks, wait):
        total = None
        for step in range(steps):
            at = slice(step * block, (step + 1) * block)
            left = jnp.concatenate([ref[:, at] for ref in ins], axis=0)
            product = mxu(left, blocks[step], 1, 0)
            total = product if total is None else total + product
        total = total.astype(jnp.bfloat16)
        for core, out_ref in enumerate(outs):
            for index in range(count):
                at = index * length + core * rows
                out_ref[index * rows : (index + 1) * rows] = total[at : at + rows]

    outs = [(count * rows, columns) for _ in range(cores)]
    flops = 2 * count * length * depth * columns
    return call(kernel, heads, held, outs, [], False, flops)


def back_columns(grad_ref, outs, held, picked, steps):
    depth = held.shape[1]
    units = held.shape[0] // steps
    rows = grad_ref.shape[0] // len(outs)
    for place, step in enumerate(picked):
        total = None
        for unit in range(units):
            grads = grad_ref[:, unit * UNIT : (unit + 1) * UNIT]
            product = mxu(grads, held[unit * steps + step], 1, 1)
            total = product if total is None else total + product
        total = total.astype(jnp.bfloat16)
        for core, out_ref in enumerate(outs):
            out_ref[:, place * depth : (place + 1) * depth] = total[
                core * rows : (core + 1) * rows
            ]


def back_first(qkv, terms, held, start, cores, picked, steps):
    length, merged = qkv.shape
    rows = length // cores

    def kernel(ins, outs, blocks, wait):
        start = ins[0][0]
        masked = later_keys(length, start)
        ranges = []
        for core in range(cores):
            at = start + core * rows
            at = jnp.where(at >= length, at - length, at)
            ranges.append(pl.ds(pl.multiple_of(at, rows), rows))
        rolled = jnp.concatenate([ins[1][part] for part in ranges], axis=0)
        for unit in range(merged // UNIT):
            at = unit * UNIT
            part = slice(unit * GROUP * HD, (unit + 1) * GROUP * HD)
            grads = ins[2][:, part].astype(jnp.float32)
            for ref in ins[3:]:
                grads = grads + ref[:, part].astype(jnp.float32)
            attend_back_unit(
                rolled[:, at : at + UNIT], grads.astype(jnp.bfloat16), masked, outs[0], at
            )
        back_columns(outs[0], outs[1:], blocks, picked, steps)

    columns = len(picked) * held.shape[1]
    outs = [qkv.shape] + [(rows, columns) for _ in range(cores)]
    flops = 2 * length * merged * columns
    results = call(kernel, [start, qkv] + terms, held, outs, [], False, flops)
    return results[0], results[1:]


def back_rest(grad_qkv, held, cores, picked, steps):
    length, merged = grad_qkv.shape

    def kernel(ins, outs, blocks, wait):
        back_columns(ins[0], outs, blocks, picked, steps)

    columns = len(picked) * held.shape[1]
    outs = [(length // cores, columns) for _ in range(cores)]
    flops = 2 * length * merged * columns
    return call(kernel, [grad_qkv], held, outs, [], False, flops)


def add_landed(words, residual, pieces):
    columns = pieces[0].shape[1]

    def kernel(words_ref, residual_ref, *refs):
        out_ref = refs[-1]
        for step, piece_ref in enumerate(refs[:-1]):
            at = pl.ds(pl.multiple_of(words_ref[1 + step], columns), columns)
            total = residual_ref[:, at].astype(jnp.float32) + piece_ref[...].astype(jnp.float32)
            out_ref[:, at] = total.astype(jnp.bfloat16)

    return pl.pallas_call(
        kernel,
        in_specs=[SCALAR] + [LOCAL for _ in range(1 + len(pieces))],
        out_specs=LOCAL,
        out_shape=jax.ShapeDtypeStruct(residual.shape, jnp.bfloat16),
        compiler_params=pltpu.CompilerParams(vmem_limit_bytes=8 << 20),
        name="add_landed",
    )(words, residual, *pieces)


def per_device(x_fwd, x_bwd, grad_out, saved_qkv, norm_gain, w_qkv, w_out):
    return window(
        x_fwd[0, 0],
        x_bwd[0, 0],
        grad_out[0, 0],
        saved_qkv[0, 0],
        norm_gain,
        w_qkv[0],
        w_out[0],
    )


def window(fwd_rows, bwd_rows, grad_rows, qkv_saved, gain_row, weight_qkv, weight_out):
    rows, width = fwd_rows.shape
    cores = lax.axis_size("tensor")
    replicas = lax.axis_size("dp")
    columns = weight_out.shape[1]
    places = jnp.bitwise_xor(lax.axis_index("dp"), jnp.arange(replicas, dtype=jnp.int32)) * columns
    words = jnp.concatenate([jnp.full((1,), lax.axis_index("tensor") * rows), places])
    if replicas != 4:
        raise ValueError("dp size")

    def grad_piece(step):
        at = jnp.bitwise_xor(lax.axis_index("dp"), step) * columns
        return lax.dynamic_slice_in_dim(grad_rows, at, columns, axis=1)

    pieces = [grad_piece(0)]
    pieces += [over_dp(grad_piece(step), step) for step in range(1, replicas)]

    normed_rows = normalize(fwd_rows, gain_row)
    normed_far = over_dp(normed_rows, 2)
    normed_near = over_dp(normed_rows, 1)
    own_heads, held = forward_heads(blocks_of_cores(normed_rows), weight_qkv, None, words)
    far_heads = forward_heads(blocks_of_cores(normed_far), weight_qkv, held, words)
    near_heads = forward_heads(blocks_of_cores(normed_near), weight_qkv, held, words)
    last_heads = over_dp(far_heads, 1)

    exchanged = [blocks_of_cores(piece) for piece in pieces]
    terms, held_out = head_terms(exchanged, weight_out)
    relay = over_dp(terms[3], 1)
    near = over_dp(terms[1], 1)
    joined = (terms[2].astype(jnp.float32) + relay.astype(jnp.float32)).astype(jnp.bfloat16)
    terms = [terms[0], near, over_dp(joined, 2)]

    fwd_prev = over_pipe(fwd_rows, 1)
    bwd_next = over_pipe(bwd_rows, -1)
    grad_next = over_pipe(grad_rows, -1)

    steps = width // held.shape[1]
    first, rest = range(steps // 2), range(steps // 2, steps)
    half = len(first) * held.shape[1]
    grad_qkv, (keep, *sends) = back_first(qkv_saved, terms, held, words, cores, first, steps)
    scaled = sum_over_cores(keep, sends) * gain_row[:, :half]
    arrived = [over_pipe(scaled.astype(jnp.bfloat16), -1)]
    keep, *sends = back_rest(grad_qkv, held, cores, rest, steps)
    scaled = sum_over_cores(keep, sends) * gain_row[:, half:]
    arrived.append(over_pipe(scaled.astype(jnp.bfloat16), -1))
    scaled = jnp.concatenate(arrived, axis=1).astype(jnp.float32)
    grad_input = norm_back(bwd_next, grad_next, scaled)

    landed = {}
    groups = (((0, 1, 2), [own_heads, near_heads, far_heads]), ((3,), [last_heads]))
    for group, heads in groups:
        keep, *sends = project(heads, held_out, cores)
        summed = sum_over_cores(keep, sends).astype(jnp.bfloat16)
        for index, step in enumerate(group):
            landed[step] = lax.ppermute(
                summed[index * rows : (index + 1) * rows],
                ("pipe", "dp"),
                cross_pairs(step, 1),
            )
    output = add_landed(words, fwd_prev, [landed[step] for step in range(replicas)])
    return (output[None, None], grad_input[None, None])


def solution(mesh):
    return jax.shard_map(
        per_device,
        mesh=mesh,
        in_specs=(
            P("pipe", "dp", "tensor", None),
            P("pipe", "dp", "tensor", None),
            P("pipe", "dp", "tensor", None),
            P("pipe", "dp", None, "tensor"),
            P("pipe", None),
            P("pipe", None, "tensor"),
            P("pipe", "tensor", "dp"),
        ),
        out_specs=(P("pipe", "dp", "tensor", None), P("pipe", "dp", "tensor", None)),
        check_vma=False,
    )
```

```python
import math

import jax
import jax.numpy as jnp
from jax import lax
from jax.experimental import pallas as pl
from jax.experimental.pallas import tpu as pltpu
from jax.sharding import PartitionSpec as P


HD = 128
GROUP = 6
UNIT = (GROUP + 2) * HD


def shift_pairs(count, steps):
    return [(source, (source + steps) % count) for source in range(count)]


def partner_pairs(count, step):
    if count & (count - 1):
        raise ValueError("dp size")
    return [(source, source ^ step) for source in range(count)]


def cross_pairs(step, forward):
    pipes = lax.axis_size("pipe")
    count = lax.axis_size("dp")
    return [
        (p * count + d, ((p + forward) % pipes) * count + (d ^ step))
        for p in range(pipes)
        for d in range(count)
    ]


def over_dp(value, step):
    return lax.ppermute(value, "dp", partner_pairs(lax.axis_size("dp"), step))


def over_pipe(value, steps):
    return lax.ppermute(value, "pipe", shift_pairs(lax.axis_size("pipe"), steps))


def blocks_of_cores(value):
    count = lax.axis_size("tensor")
    return [value] + [
        lax.ppermute(value, "tensor", shift_pairs(count, -step)) for step in range(1, count)
    ]


def sum_over_cores(keep, sends):
    count = lax.axis_size("tensor")
    total = keep.astype(jnp.float32)
    for step in range(1, count):
        block = lax.ppermute(sends[step - 1], "tensor", shift_pairs(count, step))
        total = total + block.astype(jnp.float32)
    return total


def normalize(inputs, gain_row):
    widened = inputs.astype(jnp.float32)
    inverse = lax.rsqrt(jnp.mean(widened * widened, axis=-1, keepdims=True) + 1e-05)
    return (widened * inverse * gain_row).astype(jnp.bfloat16)


def norm_back(inputs, grad_rows, scaled):
    widened = inputs.astype(jnp.float32)
    inverse = lax.rsqrt(jnp.mean(widened * widened, axis=-1, keepdims=True) + 1e-05)
    middle = jnp.mean(widened * scaled, axis=-1, keepdims=True)
    result = (
        grad_rows.astype(jnp.float32)
        + inverse * scaled
        - widened * inverse * inverse * inverse * middle
    )
    return result.astype(jnp.bfloat16)


def mxu(left, right, left_dim, right_dim):
    return lax.dot_general(
        left,
        right,
        (((left_dim,), (right_dim,)), ((), ())),
        preferred_element_type=jnp.float32,
    )


def later_keys(length, start):
    rows_at = lax.broadcasted_iota(jnp.int32, (length, length), 0) + start
    cols_at = lax.broadcasted_iota(jnp.int32, (length, length), 1) + start
    rows_at = jnp.where(rows_at >= length, rows_at - length, rows_at)
    cols_at = jnp.where(cols_at >= length, cols_at - length, cols_at)
    return cols_at > rows_at


def head_columns(value, head):
    return value[:, head * HD : (head + 1) * HD]


def stacked_heads(value):
    return jnp.concatenate([head_columns(value, g) for g in range(GROUP)], axis=0)


def probabilities(queries, keys, masked):
    length = keys.shape[0]
    scores = mxu(queries, keys, 1, 1) * (1.0 / math.sqrt(HD))
    rows = []
    for g in range(GROUP):
        part = jnp.where(masked, -1e30, scores[g * length : (g + 1) * length])
        part = jnp.exp(part - jnp.max(part, axis=-1, keepdims=True))
        rows.append(part / jnp.sum(part, axis=-1, keepdims=True))
    return jnp.concatenate(rows, axis=0)


def attend_unit(qkv, masked, out_ref, at):
    length = qkv.shape[0]
    keys, values = head_columns(qkv, GROUP), head_columns(qkv, GROUP + 1)
    probs = probabilities(stacked_heads(qkv), keys, masked).astype(jnp.bfloat16)
    heads = mxu(probs, values, 1, 0).astype(jnp.bfloat16)
    for g in range(GROUP):
        out_ref[:, at + g * HD : at + (g + 1) * HD] = heads[g * length : (g + 1) * length]


def attend_back_unit(qkv, grads, masked, out_ref, at):
    length = qkv.shape[0]
    factor = 1.0 / math.sqrt(HD)
    keys, values = head_columns(qkv, GROUP), head_columns(qkv, GROUP + 1)
    queries = stacked_heads(qkv)
    grads = stacked_heads(grads)
    probs = probabilities(queries, keys, masked)
    grad_values = mxu(probs.astype(jnp.bfloat16), grads, 0, 0)
    grad_probs = mxu(grads, values, 1, 1)
    grad_scores = probs * (grad_probs - jnp.sum(probs * grad_probs, axis=-1, keepdims=True))
    grad_scores = grad_scores.astype(jnp.bfloat16)
    grad_queries = mxu(grad_scores, keys, 1, 0) * factor
    grad_keys = mxu(grad_scores, queries, 0, 0) * factor
    for g in range(GROUP):
        out_ref[:, at + g * HD : at + (g + 1) * HD] = grad_queries[
            g * length : (g + 1) * length
        ].astype(jnp.bfloat16)
    out_ref[:, at + GROUP * HD : at + (GROUP + 1) * HD] = grad_keys.astype(jnp.bfloat16)
    out_ref[:, at + (GROUP + 1) * HD : at + UNIT] = grad_values.astype(jnp.bfloat16)


def divisor(size, most):
    parts = 1
    while size % parts or size // parts > most or (size // parts) % HD:
        parts += 1
        if parts > size:
            raise ValueError("block size")
    return size // parts


SCALAR = pl.BlockSpec(memory_space=pltpu.SMEM)
LOCAL = pl.BlockSpec(memory_space=pltpu.VMEM)
REMOTE = pl.BlockSpec(memory_space=pltpu.HBM)


def call(kernel, args, weight, helds, outs, blocks, keep, flops):
    count = len(args)
    extra = 1 if blocks else len(helds)
    shape = (len(blocks), blocks[0][0].size, blocks[0][1].size) if blocks else ()
    moved = 2 * math.prod(shape) if blocks else 0

    def body(*refs):
        ins, weight_refs = refs[:count], refs[count : count + extra]
        results = refs[count + extra : count + extra + len(outs)]
        if not blocks:
            places = [ref.at[index] for ref in weight_refs for index in range(ref.shape[0])]
            kernel(ins, results, lambda index: places[index][...])
            return
        held, sems = refs[count + extra + len(outs) :]
        moves = [
            pltpu.make_async_copy(weight_refs[0].at[part], held.at[index], sems.at[index])
            for index, part in enumerate(blocks)
        ]
        for move in moves:
            move.start()

        def loaded(index):
            moves[index].wait()
            return held[index]

        kernel(ins, results, loaded)

    out_specs = [LOCAL for _ in outs]
    out_shape = [
        out if hasattr(out, "dtype") else jax.ShapeDtypeStruct(out, jnp.bfloat16) for out in outs
    ]
    scratch = []
    if blocks:
        scratch = [pltpu.SemaphoreType.DMA((len(blocks),))]
        if keep:
            out_specs.append(LOCAL)
            out_shape.append(pltpu.VMEM(shape, jnp.bfloat16))
        else:
            scratch.insert(0, pltpu.VMEM(shape, jnp.bfloat16))
        weights = [pltpu.with_memory_space_constraint(weight, pltpu.HBM)]
    else:
        weights = [pltpu.with_memory_space_constraint(held, pltpu.VMEM) for held in helds]
    limit = (0 if keep else moved) + (8 << 20)
    return pl.pallas_call(
        body,
        in_specs=[SCALAR if arg.dtype == jnp.int32 else LOCAL for arg in args]
        + [REMOTE if blocks else LOCAL for _ in weights],
        out_specs=out_specs,
        out_shape=out_shape,
        scratch_shapes=scratch,
        compiler_params=pltpu.CompilerParams(vmem_limit_bytes=limit),
        cost_estimate=pl.CostEstimate(flops=flops, bytes_accessed=moved, transcendentals=0),
    )(*args, *weights)


def row_blocks(size, columns, most):
    block = divisor(size, most)
    return [(pl.ds(row, block), pl.ds(0, columns)) for row in range(0, size, block)]


def forward_heads(batches, weight, helds, start):
    rows, width = batches[0][0].shape
    length = rows * len(batches[0])
    flat = [part for parts in batches for part in parts]
    depth = divisor(width, 1024)
    steps = width // depth
    units = sum(held.shape[0] for held in helds) // steps if helds else weight.shape[1] // UNIT

    def kernel(ins, outs, block):
        masked = later_keys(length, ins[0][0])
        for unit in range(units):
            total = None
            for step in range(steps):
                at = slice(step * depth, (step + 1) * depth)
                left = jnp.concatenate([ref[:, at] for ref in ins[1:]], axis=0)
                product = mxu(left, block(unit * steps + step), 1, 0)
                total = product if total is None else total + product
            total = total.astype(jnp.bfloat16)
            for index, out_ref in enumerate(outs):
                qkv = total[index * length : (index + 1) * length]
                attend_unit(qkv, masked, out_ref, unit * GROUP * HD)

    blocks = []
    if not helds:
        blocks = [
            (pl.ds(step * depth, depth), pl.ds(unit * UNIT, UNIT))
            for unit in range(units)
            for step in range(steps)
        ]
    flops = 2 * length * len(batches) * width * units * UNIT
    outs = [(length, units * GROUP * HD) for _ in batches]
    return call(kernel, [start] + flat, weight, helds, outs, blocks, not helds, flops)


def column_parts(depth):
    first = GROUP * HD
    return [(0, first), (first, depth)] if depth > first else [(0, depth)]


def head_terms(pieces, weight, whole):
    rows, columns = pieces[0][0].shape
    length = rows * len(pieces[0])
    depth = weight.shape[0]
    flat = [part for parts in pieces for part in parts]
    blocks = row_blocks(depth, columns, 768)
    block = depth // len(blocks)
    places = [(k, 0, depth) for k in range(whole)]
    for first, last in column_parts(depth):
        places += [(k, first, last) for k in range(whole, len(pieces))]

    def kernel(ins, outs, loaded):
        left = jnp.concatenate([ref[...] for ref in ins], axis=0)
        for step in range(len(blocks)):
            product = mxu(left, loaded(step), 1, 1).astype(jnp.bfloat16)
            at = step * block
            for (k, first, last), out_ref in zip(places, outs):
                if first <= at < last:
                    out_ref[:, at - first : at - first + block] = product[
                        k * length : (k + 1) * length
                    ]

    outs = [(length, last - first) for _, first, last in places]
    flops = 2 * len(pieces) * length * depth * columns
    *terms, held = call(kernel, flat, weight, [], outs, blocks, True, flops)
    return terms, held


def project(heads, held, cores):
    length = heads[0].shape[0]
    count, (steps, block, columns) = len(heads), held.shape
    rows = length // cores

    def kernel(ins, outs, held_block):
        total = None
        for step in range(steps):
            at = slice(step * block, (step + 1) * block)
            left = jnp.concatenate([ref[:, at] for ref in ins], axis=0)
            product = mxu(left, held_block(step), 1, 0)
            total = product if total is None else total + product
        total = total.astype(jnp.bfloat16)
        for core, out_ref in enumerate(outs):
            for index in range(count):
                at = index * length + core * rows
                out_ref[index * rows : (index + 1) * rows] = total[at : at + rows]

    outs = [(count * rows, columns) for _ in range(cores)]
    flops = 2 * count * length * steps * block * columns
    return call(kernel, heads, None, [held], outs, [], False, flops)


def rolled_rows(ref, start, cores):
    length = ref.shape[0]
    rows = length // cores
    ranges = []
    for core in range(cores):
        at = start + core * rows
        at = jnp.where(at >= length, at - length, at)
        ranges.append(pl.ds(pl.multiple_of(at, rows), rows))
    return lambda columns: jnp.concatenate([ref[part, columns] for part in ranges], axis=0)


def back_units(start_ref, qkv_ref, own_ref, landed, grad_ref, units, cores):
    masked = later_keys(qkv_ref.shape[0], start_ref[0])
    saved = rolled_rows(qkv_ref, start_ref[0], cores)
    wide = GROUP * HD
    for place, unit in enumerate(units):
        grads = own_ref[:, unit * wide : (unit + 1) * wide].astype(jnp.float32)
        for ref in landed:
            grads = grads + ref[:, place * wide : (place + 1) * wide].astype(jnp.float32)
        attend_back_unit(
            saved(slice(unit * UNIT, (unit + 1) * UNIT)),
            grads.astype(jnp.bfloat16),
            masked,
            grad_ref,
            place * UNIT,
        )


def back_product(grad_ref, block, units, step, steps):
    total = None
    for place, unit in enumerate(units):
        grads = grad_ref[:, place * UNIT : (place + 1) * UNIT]
        product = mxu(grads, block(unit * steps + step), 1, 1)
        total = product if total is None else total + product
    return total


def back_early(qkv, own, landed, helds, start, cores, units, steps):
    length = qkv.shape[0]
    depth = helds[0].shape[1]

    def kernel(ins, outs, block):
        back_units(ins[0], ins[1], ins[2], ins[3:], outs[0], units, cores)
        for step in range(steps):
            outs[1][:, step * depth : (step + 1) * depth] = back_product(
                outs[0], block, units, step, steps
            )

    wide = len(units) * UNIT
    outs = [(length, wide), jax.ShapeDtypeStruct((length, steps * depth), jnp.float32)]
    flops = 2 * length * wide * steps * depth
    args = [start, qkv, own] + landed
    return call(kernel, args, None, helds, outs, [], False, flops)[1]


def back_columns(grad_ref, early, outs, block, units, picked, steps, depth):
    rows = grad_ref.shape[0] // len(outs)
    for place, step in enumerate(picked):
        total = back_product(grad_ref, block, units, step, steps)
        for ref in early:
            total = total + ref[:, step * depth : (step + 1) * depth]
        total = total.astype(jnp.bfloat16)
        for core, out_ref in enumerate(outs):
            out_ref[:, place * depth : (place + 1) * depth] = total[
                core * rows : (core + 1) * rows
            ]


def back_first(qkv, own, landed, early, helds, start, cores, units, picked, steps):
    length = qkv.shape[0]
    rows = length // cores
    depth = helds[0].shape[1]
    count = 3 + len(landed)

    def kernel(ins, outs, block):
        back_units(ins[0], ins[1], ins[2], ins[3:count], outs[0], units, cores)
        back_columns(outs[0], ins[count:], outs[1:], block, units, picked, steps, depth)

    wide = len(units) * UNIT
    columns = len(picked) * depth
    outs = [(length, wide)] + [(rows, columns) for _ in range(cores)]
    flops = 2 * length * wide * columns
    args = [start, qkv, own] + landed + early
    results = call(kernel, args, None, helds, outs, [], False, flops)
    return results[0], results[1:]


def back_rest(grad_qkv, early, helds, cores, units, picked, steps):
    length, wide = grad_qkv.shape
    depth = helds[0].shape[1]

    def kernel(ins, outs, block):
        back_columns(ins[0], ins[1:], outs, block, units, picked, steps, depth)

    columns = len(picked) * depth
    outs = [(length // cores, columns) for _ in range(cores)]
    flops = 2 * length * wide * columns
    return call(kernel, [grad_qkv] + early, None, helds, outs, [], False, flops)


def add_landed(words, residual, pieces):
    columns = pieces[0].shape[1]

    def kernel(words_ref, residual_ref, *refs):
        out_ref = refs[-1]
        for step, piece_ref in enumerate(refs[:-1]):
            at = pl.ds(pl.multiple_of(words_ref[1 + step], columns), columns)
            total = residual_ref[:, at].astype(jnp.float32) + piece_ref[...].astype(jnp.float32)
            out_ref[:, at] = total.astype(jnp.bfloat16)

    return pl.pallas_call(
        kernel,
        in_specs=[SCALAR] + [LOCAL for _ in range(1 + len(pieces))],
        out_specs=LOCAL,
        out_shape=jax.ShapeDtypeStruct(residual.shape, jnp.bfloat16),
        compiler_params=pltpu.CompilerParams(vmem_limit_bytes=8 << 20),
        name="add_landed",
    )(words, residual, *pieces)


def per_device(x_fwd, x_bwd, grad_out, saved_qkv, norm_gain, w_qkv, w_out):
    return window(
        x_fwd[0, 0],
        x_bwd[0, 0],
        grad_out[0, 0],
        saved_qkv[0, 0],
        norm_gain,
        w_qkv[0],
        w_out[0],
    )


def window(fwd_rows, bwd_rows, grad_rows, qkv_saved, gain_row, weight_qkv, weight_out):
    rows, width = fwd_rows.shape
    cores = lax.axis_size("tensor")
    replicas = lax.axis_size("dp")
    columns = weight_out.shape[1]
    places = jnp.bitwise_xor(lax.axis_index("dp"), jnp.arange(replicas, dtype=jnp.int32)) * columns
    words = jnp.concatenate([jnp.full((1,), lax.axis_index("tensor") * rows), places])
    if replicas != 4:
        raise ValueError("dp size")

    def grad_piece(step):
        at = jnp.bitwise_xor(lax.axis_index("dp"), step) * columns
        return lax.dynamic_slice_in_dim(grad_rows, at, columns, axis=1)

    pieces = [grad_piece(0)]
    pieces += [over_dp(grad_piece(step), step) for step in range(1, replicas)]

    normed_rows = normalize(fwd_rows, gain_row)
    normed_far = over_dp(normed_rows, 2)
    normed_near = over_dp(normed_rows, 1)
    own_parts = blocks_of_cores(normed_rows)
    own_heads, *helds = forward_heads([own_parts], weight_qkv, [], words)
    near_parts = blocks_of_cores(normed_near)
    far_parts = blocks_of_cores(normed_far)
    near_heads, far_heads = forward_heads([near_parts, far_parts], None, helds, words)
    last_heads = over_dp(far_heads, 1)

    exchanged = [blocks_of_cores(piece) for piece in pieces]
    (own, *rest), held_out = head_terms(exchanged, weight_out, 1)
    landed = []
    for index in range(len(rest) // 3):
        near, far, relay = rest[3 * index : 3 * index + 3]
        near = over_dp(near, 1)
        relay = over_dp(relay, 1)
        far = (far.astype(jnp.float32) + relay.astype(jnp.float32)).astype(jnp.bfloat16)
        landed.append([near, over_dp(far, 2)])

    fwd_prev = over_pipe(fwd_rows, 1)
    bwd_next = over_pipe(bwd_rows, -1)
    grad_next = over_pipe(grad_rows, -1)

    depth = helds[0].shape[1]
    steps = width // depth
    some = steps - max(1, steps // 4)
    first, rest = range(some), range(some, steps)
    half = len(first) * depth
    units = range(qkv_saved.shape[1] // UNIT)
    early = []
    if len(landed) > 1:
        early = [back_early(qkv_saved, own, landed[0], helds, words, cores, units[:1], steps)]
        units = units[1:]
    grad_qkv, (keep, *sends) = back_first(
        qkv_saved, own, landed[-1], early, helds, words, cores, units, first, steps
    )
    scaled = sum_over_cores(keep, sends) * gain_row[:, :half]
    arrived = [over_pipe(scaled.astype(jnp.bfloat16), -1)]
    keep, *sends = back_rest(grad_qkv, early, helds, cores, units, rest, steps)
    scaled = sum_over_cores(keep, sends) * gain_row[:, half:]
    arrived.append(over_pipe(scaled.astype(jnp.bfloat16), -1))
    scaled = jnp.concatenate(arrived, axis=1).astype(jnp.float32)
    grad_input = norm_back(bwd_next, grad_next, scaled)

    pieces = {}
    groups = (((0,), [own_heads]), ((1, 2), [near_heads, far_heads]), ((3,), [last_heads]))
    for group, heads in groups:
        keep, *sends = project(heads, held_out, cores)
        summed = sum_over_cores(keep, sends).astype(jnp.bfloat16)
        for index, step in enumerate(group):
            pieces[step] = lax.ppermute(
                summed[index * rows : (index + 1) * rows],
                ("pipe", "dp"),
                cross_pairs(step, 1),
            )
    output = add_landed(words, fwd_prev, [pieces[step] for step in range(replicas)])
    return (output[None, None], grad_input[None, None])


def solution(mesh):
    return jax.shard_map(
        per_device,
        mesh=mesh,
        in_specs=(
            P("pipe", "dp", "tensor", None),
            P("pipe", "dp", "tensor", None),
            P("pipe", "dp", "tensor", None),
            P("pipe", "dp", None, "tensor"),
            P("pipe", None),
            P("pipe", None, "tensor"),
            P("pipe", "tensor", "dp"),
        ),
        out_specs=(P("pipe", "dp", "tensor", None), P("pipe", "dp", "tensor", None)),
        check_vma=False,
    )
```

```python
import math

import jax
import jax.numpy as jnp
from jax import lax
from jax.experimental import pallas as pl
from jax.experimental.pallas import tpu as pltpu
from jax.sharding import PartitionSpec as P


HD = 128
GROUP = 6
UNIT = (GROUP + 2) * HD


def shift_pairs(count, steps):
    return [(source, (source + steps) % count) for source in range(count)]


def partner_pairs(count, step):
    if count & (count - 1):
        raise ValueError("dp size")
    return [(source, source ^ step) for source in range(count)]


def cross_pairs(step, forward):
    pipes = lax.axis_size("pipe")
    count = lax.axis_size("dp")
    return [
        (p * count + d, ((p + forward) % pipes) * count + (d ^ step))
        for p in range(pipes)
        for d in range(count)
    ]


def over_dp(value, step):
    return lax.ppermute(value, "dp", partner_pairs(lax.axis_size("dp"), step))


def over_pipe(value, steps):
    return lax.ppermute(value, "pipe", shift_pairs(lax.axis_size("pipe"), steps))


def blocks_of_cores(value):
    count = lax.axis_size("tensor")
    return [value] + [
        lax.ppermute(value, "tensor", shift_pairs(count, -step)) for step in range(1, count)
    ]


def sum_over_cores(keep, sends):
    count = lax.axis_size("tensor")
    total = keep.astype(jnp.float32)
    for step in range(1, count):
        block = lax.ppermute(sends[step - 1], "tensor", shift_pairs(count, step))
        total = total + block.astype(jnp.float32)
    return total


def mxu(left, right, left_dim, right_dim):
    return lax.dot_general(
        left,
        right,
        (((left_dim,), (right_dim,)), ((), ())),
        preferred_element_type=jnp.float32,
    )


def later_keys(length, start):
    rows_at = lax.broadcasted_iota(jnp.int32, (length, length), 0) + start
    cols_at = lax.broadcasted_iota(jnp.int32, (length, length), 1) + start
    rows_at = jnp.where(rows_at >= length, rows_at - length, rows_at)
    cols_at = jnp.where(cols_at >= length, cols_at - length, cols_at)
    return cols_at > rows_at


def head_columns(value, head):
    return value[:, head * HD : (head + 1) * HD]


def stacked_heads(value):
    return jnp.concatenate([head_columns(value, g) for g in range(GROUP)], axis=0)


def probabilities(queries, keys, masked):
    length = keys.shape[0]
    scores = mxu(queries, keys, 1, 1) * (1.0 / math.sqrt(HD))
    rows = []
    for g in range(GROUP):
        part = jnp.where(masked, -1e30, scores[g * length : (g + 1) * length])
        part = jnp.exp(part - jnp.max(part, axis=-1, keepdims=True))
        rows.append(part / jnp.sum(part, axis=-1, keepdims=True))
    return jnp.concatenate(rows, axis=0)


def attend_unit(qkv, masked, out_ref, at):
    length = qkv.shape[0]
    keys, values = head_columns(qkv, GROUP), head_columns(qkv, GROUP + 1)
    probs = probabilities(stacked_heads(qkv), keys, masked).astype(jnp.bfloat16)
    heads = mxu(probs, values, 1, 0).astype(jnp.bfloat16)
    for g in range(GROUP):
        out_ref[:, at + g * HD : at + (g + 1) * HD] = heads[g * length : (g + 1) * length]


def attend_back_unit(qkv, grads, masked, out_ref, at):
    length = qkv.shape[0]
    factor = 1.0 / math.sqrt(HD)
    keys, values = head_columns(qkv, GROUP), head_columns(qkv, GROUP + 1)
    queries = stacked_heads(qkv)
    grads = stacked_heads(grads)
    probs = probabilities(queries, keys, masked)
    grad_values = mxu(probs.astype(jnp.bfloat16), grads, 0, 0)
    grad_probs = mxu(grads, values, 1, 1)
    grad_scores = probs * (grad_probs - jnp.sum(probs * grad_probs, axis=-1, keepdims=True))
    grad_scores = grad_scores.astype(jnp.bfloat16)
    grad_queries = mxu(grad_scores, keys, 1, 0) * factor
    grad_keys = mxu(grad_scores, queries, 0, 0) * factor
    for g in range(GROUP):
        out_ref[:, at + g * HD : at + (g + 1) * HD] = grad_queries[
            g * length : (g + 1) * length
        ].astype(jnp.bfloat16)
    out_ref[:, at + GROUP * HD : at + (GROUP + 1) * HD] = grad_keys.astype(jnp.bfloat16)
    out_ref[:, at + (GROUP + 1) * HD : at + UNIT] = grad_values.astype(jnp.bfloat16)


def divisor(size, most):
    parts = 1
    while size % parts or size // parts > most or (size // parts) % HD:
        parts += 1
        if parts > size:
            raise ValueError("block size")
    return size // parts


SCALAR = pl.BlockSpec(memory_space=pltpu.SMEM)
LOCAL = pl.BlockSpec(memory_space=pltpu.VMEM)
REMOTE = pl.BlockSpec(memory_space=pltpu.HBM)


def call(kernel, args, weight, helds, outs, blocks, keep, flops, temps=(), fetch=()):
    count = len(args)
    extra = 1 if blocks else len(helds)
    shape = (len(blocks), blocks[0][0].size, blocks[0][1].size) if blocks else ()
    moved = 2 * math.prod(shape) if blocks else 0

    def body(*refs):
        split = len(refs) - len(temps)
        refs, rest = refs[:split], refs[split:]
        ins, weight_refs = list(refs[:count]), refs[count : count + extra]
        if fetch:
            *landing, fetch_sems = refs[len(refs) - len(fetch) - 1 :]
            refs = refs[: len(refs) - len(fetch) - 1]
            fetches = [
                pltpu.make_async_copy(ins[index], ref, fetch_sems.at[place])
                for place, (index, ref) in enumerate(zip(fetch, landing))
            ]
            for move in fetches:
                move.start()
            for move, index, ref in zip(fetches, fetch, landing):
                move.wait()
                ins[index] = ref
        results = refs[count + extra : count + extra + len(outs)]
        if not blocks:
            places = [ref.at[index] for ref in weight_refs for index in range(ref.shape[0])]
            kernel(ins, results, lambda index: places[index][...], *rest)
            return
        held, sems = refs[count + extra + len(outs) :]
        moves = [
            pltpu.make_async_copy(weight_refs[0].at[part], held.at[index], sems.at[index])
            for index, part in enumerate(blocks)
        ]
        for move in moves:
            move.start()

        def loaded(index):
            moves[index].wait()
            return held[index]

        kernel(ins, results, loaded, *rest)

    out_specs = [LOCAL for _ in outs]
    out_shape = [
        out if hasattr(out, "dtype") else jax.ShapeDtypeStruct(out, jnp.bfloat16) for out in outs
    ]
    scratch = []
    if blocks:
        scratch = [pltpu.SemaphoreType.DMA((len(blocks),))]
        if keep:
            out_specs.append(LOCAL)
            out_shape.append(pltpu.VMEM(shape, jnp.bfloat16))
        else:
            scratch.insert(0, pltpu.VMEM(shape, jnp.bfloat16))
        weights = [pltpu.with_memory_space_constraint(weight, pltpu.HBM)]
    else:
        weights = [pltpu.with_memory_space_constraint(held, pltpu.VMEM) for held in helds]
    if fetch:
        scratch += [pltpu.VMEM(args[index].shape, args[index].dtype) for index in fetch]
        scratch.append(pltpu.SemaphoreType.DMA((len(fetch),)))
        args = [
            pltpu.with_memory_space_constraint(arg, pltpu.HBM) if index in fetch else arg
            for index, arg in enumerate(args)
        ]
    specs = [SCALAR if arg.dtype == jnp.int32 else LOCAL for arg in args]
    for index in fetch:
        specs[index] = REMOTE
    limit = (0 if keep else moved) + (8 << 20)
    return pl.pallas_call(
        body,
        in_specs=specs + [REMOTE if blocks else LOCAL for _ in weights],
        out_specs=out_specs,
        out_shape=out_shape,
        scratch_shapes=scratch + list(temps),
        compiler_params=pltpu.CompilerParams(vmem_limit_bytes=limit),
        cost_estimate=pl.CostEstimate(flops=flops, bytes_accessed=moved, transcendentals=0),
    )(*args, *weights)


def row_blocks(size, columns, most):
    block = divisor(size, most)
    return [(pl.ds(row, block), pl.ds(0, columns)) for row in range(0, size, block)]


def normalize_rows(ref, gain_ref, out_ref, first):
    step = 16 if ref.shape[0] % 16 == 0 else ref.shape[0]
    for at in range(0, ref.shape[0], step):
        wide = ref[at : at + step].astype(jnp.float32)
        inverse = lax.rsqrt(jnp.mean(wide * wide, axis=-1, keepdims=True) + 1e-05)
        normed = (wide * inverse * gain_ref[...]).astype(jnp.bfloat16)
        out_ref[first + at : first + at + step] = normed


def forward_heads(batches, weight, helds, start, gain, fetch):
    rows, width = batches[0][0].shape
    length = rows * len(batches[0])
    flat = [part for parts in batches for part in parts]
    depth = divisor(width, 1024)
    steps = width // depth
    units = sum(held.shape[0] for held in helds) // steps if helds else weight.shape[1] // UNIT

    def kernel(ins, outs, block, normed_ref):
        for index, ref in enumerate(ins[2:]):
            normalize_rows(ref, ins[1], normed_ref, index * rows)
        masked = later_keys(length, ins[0][0])
        for unit in range(units):
            total = None
            for step in range(steps):
                left = normed_ref[:, step * depth : (step + 1) * depth]
                product = mxu(left, block(unit * steps + step), 1, 0)
                total = product if total is None else total + product
            total = total.astype(jnp.bfloat16)
            for index, out_ref in enumerate(outs):
                qkv = total[index * length : (index + 1) * length]
                attend_unit(qkv, masked, out_ref, unit * GROUP * HD)

    blocks = []
    if not helds:
        blocks = [
            (pl.ds(step * depth, depth), pl.ds(unit * UNIT, UNIT))
            for unit in range(units)
            for step in range(steps)
        ]
    flops = 2 * length * len(batches) * width * units * UNIT
    outs = [(length, units * GROUP * HD) for _ in batches]
    temps = [pltpu.VMEM((length * len(batches), width), jnp.bfloat16)]
    args = [start, gain] + flat
    keep = not helds
    return call(kernel, args, weight, helds, outs, blocks, keep, flops, temps, fetch)


def column_parts(depth):
    first = GROUP * HD
    return [(0, first), (first, depth)] if depth > first else [(0, depth)]


def head_terms(pieces, weight, whole):
    rows, columns = pieces[0][0].shape
    length = rows * len(pieces[0])
    depth = weight.shape[0]
    flat = [part for parts in pieces for part in parts]
    blocks = row_blocks(depth, columns, 768)
    block = depth // len(blocks)
    places = [(k, 0, depth) for k in range(whole)]
    for first, last in column_parts(depth):
        places += [(k, first, last) for k in range(whole, len(pieces))]

    def kernel(ins, outs, loaded):
        left = jnp.concatenate([ref[...] for ref in ins], axis=0)
        for step in range(len(blocks)):
            product = mxu(left, loaded(step), 1, 1).astype(jnp.bfloat16)
            at = step * block
            for (k, first, last), out_ref in zip(places, outs):
                if first <= at < last:
                    out_ref[:, at - first : at - first + block] = product[
                        k * length : (k + 1) * length
                    ]

    outs = [(length, last - first) for _, first, last in places]
    flops = 2 * len(pieces) * length * depth * columns
    *terms, held = call(kernel, flat, weight, [], outs, blocks, True, flops)
    return terms, held


def project(heads, held, cores):
    length = heads[0].shape[0]
    count, (steps, block, columns) = len(heads), held.shape
    rows = length // cores

    def kernel(ins, outs, held_block):
        total = None
        for step in range(steps):
            at = slice(step * block, (step + 1) * block)
            left = jnp.concatenate([ref[:, at] for ref in ins], axis=0)
            product = mxu(left, held_block(step), 1, 0)
            total = product if total is None else total + product
        total = total.astype(jnp.bfloat16)
        for core, out_ref in enumerate(outs):
            for index in range(count):
                at = index * length + core * rows
                out_ref[index * rows : (index + 1) * rows] = total[at : at + rows]

    outs = [(count * rows, columns) for _ in range(cores)]
    flops = 2 * count * length * steps * block * columns
    return call(kernel, heads, None, [held], outs, [], False, flops)


def rolled_rows(ref, start, cores):
    length = ref.shape[0]
    rows = length // cores
    ranges = []
    for core in range(cores):
        at = start + core * rows
        at = jnp.where(at >= length, at - length, at)
        ranges.append(pl.ds(pl.multiple_of(at, rows), rows))
    return lambda columns: jnp.concatenate([ref[part, columns] for part in ranges], axis=0)


def back_units(start_ref, qkv_ref, own_ref, landed, grad_ref, units, cores):
    masked = later_keys(qkv_ref.shape[0], start_ref[0])
    saved = rolled_rows(qkv_ref, start_ref[0], cores)
    wide = GROUP * HD
    for place, unit in enumerate(units):
        grads = own_ref[:, unit * wide : (unit + 1) * wide].astype(jnp.float32)
        for ref in landed:
            grads = grads + ref[:, place * wide : (place + 1) * wide].astype(jnp.float32)
        attend_back_unit(
            saved(slice(unit * UNIT, (unit + 1) * UNIT)),
            grads.astype(jnp.bfloat16),
            masked,
            grad_ref,
            place * UNIT,
        )


def back_product(grad_ref, block, units, step, steps):
    total = None
    for place, unit in enumerate(units):
        grads = grad_ref[:, place * UNIT : (place + 1) * UNIT]
        product = mxu(grads, block(unit * steps + step), 1, 1)
        total = product if total is None else total + product
    return total


def back_early(qkv, own, landed, helds, start, cores, units, steps):
    length = qkv.shape[0]
    depth = helds[0].shape[1]

    def kernel(ins, outs, block):
        back_units(ins[0], ins[1], ins[2], ins[3:], outs[0], units, cores)
        for step in range(steps):
            outs[1][:, step * depth : (step + 1) * depth] = back_product(
                outs[0], block, units, step, steps
            )

    wide = len(units) * UNIT
    outs = [(length, wide), jax.ShapeDtypeStruct((length, steps * depth), jnp.float32)]
    flops = 2 * length * wide * steps * depth
    args = [start, qkv, own] + landed
    return call(kernel, args, None, helds, outs, [], False, flops)[1]


def back_columns(grad_ref, early, outs, block, units, picked, steps, depth):
    rows = grad_ref.shape[0] // len(outs)
    for place, step in enumerate(picked):
        total = back_product(grad_ref, block, units, step, steps)
        for ref in early:
            total = total + ref[:, step * depth : (step + 1) * depth]
        total = total.astype(jnp.bfloat16)
        for core, out_ref in enumerate(outs):
            out_ref[:, place * depth : (place + 1) * depth] = total[
                core * rows : (core + 1) * rows
            ]


def back_first(qkv, own, landed, early, helds, start, cores, units, picked, steps):
    length = qkv.shape[0]
    rows = length // cores
    depth = helds[0].shape[1]
    count = 3 + len(landed)

    def kernel(ins, outs, block):
        back_units(ins[0], ins[1], ins[2], ins[3:count], outs[0], units, cores)
        back_columns(outs[0], ins[count:], outs[1:], block, units, picked, steps, depth)

    wide = len(units) * UNIT
    columns = len(picked) * depth
    outs = [(length, wide)] + [(rows, columns) for _ in range(cores)]
    flops = 2 * length * wide * columns
    args = [start, qkv, own] + landed + early
    results = call(kernel, args, None, helds, outs, [], False, flops)
    return results[0], results[1:]


def back_rest(grad_qkv, early, helds, cores, units, picked, steps):
    length, wide = grad_qkv.shape
    depth = helds[0].shape[1]

    def kernel(ins, outs, block):
        back_columns(ins[0], ins[1:], outs, block, units, picked, steps, depth)

    columns = len(picked) * depth
    outs = [(length // cores, columns) for _ in range(cores)]
    flops = 2 * length * wide * columns
    return call(kernel, [grad_qkv] + early, None, helds, outs, [], False, flops)


def norm_back(inputs, grad_rows, parts):
    rows, _ = inputs.shape
    step = 16 if rows % 16 == 0 else rows

    def kernel(inputs_ref, grad_ref, *refs):
        *part_refs, out_ref = refs
        for at in range(0, rows, step):
            wide = inputs_ref[at : at + step].astype(jnp.float32)
            scaled = [ref[at : at + step].astype(jnp.float32) for ref in part_refs]
            scaled = jnp.concatenate(scaled, axis=1)
            inverse = lax.rsqrt(jnp.mean(wide * wide, axis=-1, keepdims=True) + 1e-05)
            middle = jnp.mean(wide * scaled, axis=-1, keepdims=True)
            result = (
                grad_ref[at : at + step].astype(jnp.float32)
                + inverse * scaled
                - wide * (inverse * inverse * inverse * middle)
            )
            out_ref[at : at + step] = result.astype(jnp.bfloat16)

    return pl.pallas_call(
        kernel,
        in_specs=[LOCAL for _ in range(2 + len(parts))],
        out_specs=LOCAL,
        out_shape=jax.ShapeDtypeStruct(inputs.shape, jnp.bfloat16),
        compiler_params=pltpu.CompilerParams(vmem_limit_bytes=8 << 20),
        name="norm_back",
    )(inputs, grad_rows, *parts)


def per_device(x_fwd, x_bwd, grad_out, saved_qkv, norm_gain, w_qkv, w_out):
    return window(
        x_fwd[0, 0],
        x_bwd[0, 0],
        grad_out[0, 0],
        saved_qkv[0, 0],
        norm_gain,
        w_qkv[0],
        w_out[0],
    )


def window(fwd_rows, bwd_rows, grad_rows, qkv_saved, gain_row, weight_qkv, weight_out):
    rows, width = fwd_rows.shape
    cores = lax.axis_size("tensor")
    replicas = lax.axis_size("dp")
    columns = weight_out.shape[1]
    words = jnp.full((1,), lax.axis_index("tensor") * rows, jnp.int32)

    def columns_of(step):
        return jnp.bitwise_xor(lax.axis_index("dp"), step) * columns

    if replicas != 4:
        raise ValueError("dp size")

    def grad_piece(step):
        return lax.dynamic_slice_in_dim(grad_rows, columns_of(step), columns, axis=1)

    moved = [grad_piece(0)]
    moved += [over_dp(grad_piece(step), step) for step in range(1, replicas)]

    far_rows = over_dp(fwd_rows, 3)
    near_rows = over_dp(fwd_rows, 1)
    own_parts = blocks_of_cores(fwd_rows)
    own_heads, *helds = forward_heads([own_parts], weight_qkv, [], words, gain_row, (1, 2))
    near_parts = blocks_of_cores(near_rows)
    far_parts = blocks_of_cores(far_rows)
    near_heads, far_heads = forward_heads([near_parts, far_parts], None, helds, words, gain_row, ())
    last_heads = over_dp(far_heads, 1)

    exchanged = [blocks_of_cores(piece) for piece in moved]
    (own, *rest), held_out = head_terms(exchanged, weight_out, 1)
    landed = []
    for index in range(len(rest) // 3):
        near, far, relay = rest[3 * index : 3 * index + 3]
        near = over_dp(near, 1)
        relay = over_dp(relay, 1)
        far = (far.astype(jnp.float32) + relay.astype(jnp.float32)).astype(jnp.bfloat16)
        landed.append([near, over_dp(far, 2)])

    fwd_prev = over_pipe(fwd_rows, 1)
    bwd_next = over_pipe(bwd_rows, -1)
    grad_next = over_pipe(grad_rows, -1)

    depth = helds[0].shape[1]
    steps = width // depth
    some = steps - max(1, steps // 4)
    some = steps - max(1, steps // 2)
    first, rest = range(some), range(some, steps)
    half = len(first) * depth
    units = range(qkv_saved.shape[1] // UNIT)
    early = []
    if len(landed) > 1:
        early = [back_early(qkv_saved, own, landed[0], helds, words, cores, units[:1], steps)]
        units = units[1:]
    grad_qkv, (keep, *sends) = back_first(
        qkv_saved, own, landed[-1], early, helds, words, cores, units, first, steps
    )
    scaled = sum_over_cores(keep, sends) * gain_row[:, :half]
    arrived = [over_pipe(scaled.astype(jnp.bfloat16), -1)]
    keep, *sends = back_rest(grad_qkv, early, helds, cores, units, rest, steps)
    scaled = sum_over_cores(keep, sends) * gain_row[:, half:]
    arrived.append(over_pipe(scaled.astype(jnp.bfloat16), -1))
    grad_input = norm_back(bwd_next, grad_next, arrived)

    pieces = []
    groups = (((0,), [own_heads]), ((1, 3), [near_heads, far_heads]), ((2,), [last_heads]))
    for group, heads in groups:
        keep, *sends = project(heads, held_out, cores)
        summed = sum_over_cores(keep, sends).astype(jnp.bfloat16)
        for index, step in enumerate(group):
            piece = lax.ppermute(
                summed[index * rows : (index + 1) * rows],
                ("pipe", "dp"),
                cross_pairs(step, 1),
            )
            pieces.append((step, piece))
    output = fwd_prev
    for step, piece in reversed(pieces):
        at = columns_of(step)
        part = lax.dynamic_slice_in_dim(fwd_prev, at, columns, axis=1).astype(jnp.float32)
        part = (part + piece.astype(jnp.float32)).astype(jnp.bfloat16)
        output = lax.dynamic_update_slice_in_dim(output, part, at, axis=1)
    return (output[None, None], grad_input[None, None])


def solution(mesh):
    return jax.shard_map(
        per_device,
        mesh=mesh,
        in_specs=(
            P("pipe", "dp", "tensor", None),
            P("pipe", "dp", "tensor", None),
            P("pipe", "dp", "tensor", None),
            P("pipe", "dp", None, "tensor"),
            P("pipe", None),
            P("pipe", None, "tensor"),
            P("pipe", "tensor", "dp"),
        ),
        out_specs=(P("pipe", "dp", "tensor", None), P("pipe", "dp", "tensor", None)),
        check_vma=False,
    )
```

```python
import math

import jax
import jax.numpy as jnp
from jax import lax
from jax.experimental import pallas as pl
from jax.experimental.pallas import tpu as pltpu
from jax.sharding import PartitionSpec as P


HD = 128
GROUP = 6
UNIT = (GROUP + 2) * HD


def shift_pairs(count, steps):
    return [(source, (source + steps) % count) for source in range(count)]


def partner_pairs(count, step):
    if count & (count - 1):
        raise ValueError("dp size")
    return [(source, source ^ step) for source in range(count)]


def cross_pairs(step, forward):
    pipes = lax.axis_size("pipe")
    count = lax.axis_size("dp")
    return [
        (p * count + d, ((p + forward) % pipes) * count + (d ^ step))
        for p in range(pipes)
        for d in range(count)
    ]


def over_dp(value, step):
    return lax.ppermute(value, "dp", partner_pairs(lax.axis_size("dp"), step))


def over_pipe(value, steps):
    return lax.ppermute(value, "pipe", shift_pairs(lax.axis_size("pipe"), steps))


def blocks_of_cores(value):
    count = lax.axis_size("tensor")
    return [value] + [
        lax.ppermute(value, "tensor", shift_pairs(count, -step)) for step in range(1, count)
    ]


def sum_over_cores(keep, sends):
    count = lax.axis_size("tensor")
    total = keep.astype(jnp.float32)
    for step in range(1, count):
        block = lax.ppermute(sends[step - 1], "tensor", shift_pairs(count, step))
        total = total + block.astype(jnp.float32)
    return total


def mxu(left, right, left_dim, right_dim):
    return lax.dot_general(
        left,
        right,
        (((left_dim,), (right_dim,)), ((), ())),
        preferred_element_type=jnp.float32,
    )


def later_keys(length, start):
    rows_at = lax.broadcasted_iota(jnp.int32, (length, length), 0) + start
    cols_at = lax.broadcasted_iota(jnp.int32, (length, length), 1) + start
    rows_at = jnp.where(rows_at >= length, rows_at - length, rows_at)
    cols_at = jnp.where(cols_at >= length, cols_at - length, cols_at)
    return cols_at > rows_at


def head_columns(value, head):
    return value[:, head * HD : (head + 1) * HD]


def stacked_heads(value):
    return jnp.concatenate([head_columns(value, g) for g in range(GROUP)], axis=0)


def probabilities(queries, keys, masked):
    length = keys.shape[0]
    scores = mxu(queries, keys, 1, 1) * (math.log2(math.e) / math.sqrt(HD))
    rows = []
    for g in range(GROUP):
        part = jnp.where(masked, -1e30, scores[g * length : (g + 1) * length])
        part = jnp.exp2(part - jnp.max(part, axis=-1, keepdims=True))
        rows.append(part * (1.0 / jnp.sum(part, axis=-1, keepdims=True)))
    return jnp.concatenate(rows, axis=0)


def attend_unit(qkv, masked, out_ref, at):
    length = qkv.shape[0]
    keys, values = head_columns(qkv, GROUP), head_columns(qkv, GROUP + 1)
    probs = probabilities(stacked_heads(qkv), keys, masked).astype(jnp.bfloat16)
    heads = mxu(probs, values, 1, 0).astype(jnp.bfloat16)
    for g in range(GROUP):
        out_ref[:, at + g * HD : at + (g + 1) * HD] = heads[g * length : (g + 1) * length]


def attend_back_unit(qkv, grads, probs, out_ref, at):
    length = qkv.shape[0]
    factor = 1.0 / math.sqrt(HD)
    keys, values = head_columns(qkv, GROUP), head_columns(qkv, GROUP + 1)
    queries = stacked_heads(qkv)
    grads = stacked_heads(grads)
    grad_values = mxu(probs.astype(jnp.bfloat16), grads, 0, 0)
    grad_probs = mxu(grads, values, 1, 1)
    grad_scores = probs * (grad_probs - jnp.sum(probs * grad_probs, axis=-1, keepdims=True))
    grad_scores = grad_scores.astype(jnp.bfloat16)
    grad_queries = mxu(grad_scores, keys, 1, 0) * factor
    grad_keys = mxu(grad_scores, queries, 0, 0) * factor
    for g in range(GROUP):
        out_ref[:, at + g * HD : at + (g + 1) * HD] = grad_queries[
            g * length : (g + 1) * length
        ].astype(jnp.bfloat16)
    out_ref[:, at + GROUP * HD : at + (GROUP + 1) * HD] = grad_keys.astype(jnp.bfloat16)
    out_ref[:, at + (GROUP + 1) * HD : at + UNIT] = grad_values.astype(jnp.bfloat16)


def divisor(size, most):
    parts = 1
    while size % parts or size // parts > most or (size // parts) % HD:
        parts += 1
        if parts > size:
            raise ValueError("block size")
    return size // parts


SCALAR = pl.BlockSpec(memory_space=pltpu.SMEM)
LOCAL = pl.BlockSpec(memory_space=pltpu.VMEM)
REMOTE = pl.BlockSpec(memory_space=pltpu.HBM)


def call(kernel, args, weight, helds, outs, blocks, keep, flops, temps=(), fetch=()):
    count = len(args)
    extra = 1 if blocks else len(helds)
    shape = (len(blocks), blocks[0][0].size, blocks[0][1].size) if blocks else ()
    moved = 2 * math.prod(shape) if blocks else 0

    def body(*refs):
        split = len(refs) - len(temps)
        refs, rest = refs[:split], refs[split:]
        ins, weight_refs = list(refs[:count]), refs[count : count + extra]
        if fetch:
            *landing, fetch_sems = refs[len(refs) - len(fetch) - 1 :]
            refs = refs[: len(refs) - len(fetch) - 1]
            fetches = [
                pltpu.make_async_copy(ins[index], ref, fetch_sems.at[place])
                for place, (index, ref) in enumerate(zip(fetch, landing))
            ]
            for move in fetches:
                move.start()
            for move, index, ref in zip(fetches, fetch, landing):
                move.wait()
                ins[index] = ref
        results = refs[count + extra : count + extra + len(outs)]
        if not blocks:
            places = [ref.at[index] for ref in weight_refs for index in range(ref.shape[0])]
            kernel(ins, results, lambda index: places[index][...], *rest)
            return
        held, sems = refs[count + extra + len(outs) :]
        moves = [
            pltpu.make_async_copy(weight_refs[0].at[part], held.at[index], sems.at[index])
            for index, part in enumerate(blocks)
        ]
        for move in moves:
            move.start()

        def loaded(index):
            moves[index].wait()
            return held[index]

        kernel(ins, results, loaded, *rest)

    out_specs = [LOCAL for _ in outs]
    out_shape = [
        out if hasattr(out, "dtype") else jax.ShapeDtypeStruct(out, jnp.bfloat16) for out in outs
    ]
    scratch = []
    if blocks:
        scratch = [pltpu.SemaphoreType.DMA((len(blocks),))]
        if keep:
            out_specs.append(LOCAL)
            out_shape.append(pltpu.VMEM(shape, jnp.bfloat16))
        else:
            scratch.insert(0, pltpu.VMEM(shape, jnp.bfloat16))
        weights = [pltpu.with_memory_space_constraint(weight, pltpu.HBM) if fetch else weight]
    else:
        weights = [pltpu.with_memory_space_constraint(held, pltpu.VMEM) for held in helds]
    if fetch:
        scratch += [pltpu.VMEM(args[index].shape, args[index].dtype) for index in fetch]
        scratch.append(pltpu.SemaphoreType.DMA((len(fetch),)))
        args = [
            pltpu.with_memory_space_constraint(arg, pltpu.HBM) if index in fetch else arg
            for index, arg in enumerate(args)
        ]
    specs = [SCALAR if arg.dtype == jnp.int32 else LOCAL for arg in args]
    for index in fetch:
        specs[index] = REMOTE
    limit = (0 if keep else moved) + (8 << 20)
    return pl.pallas_call(
        body,
        in_specs=specs + [REMOTE if blocks else LOCAL for _ in weights],
        out_specs=out_specs,
        out_shape=out_shape,
        scratch_shapes=scratch + list(temps),
        compiler_params=pltpu.CompilerParams(vmem_limit_bytes=limit),
        cost_estimate=pl.CostEstimate(flops=flops, bytes_accessed=moved, transcendentals=0),
    )(*args, *weights)


def row_blocks(size, columns, most):
    block = divisor(size, most)
    return [(pl.ds(row, block), pl.ds(0, columns)) for row in range(0, size, block)]


def normalize_rows(ref, gain_ref, out_ref, first):
    step = 16 if ref.shape[0] % 16 == 0 else ref.shape[0]
    for at in range(0, ref.shape[0], step):
        wide = ref[at : at + step].astype(jnp.float32)
        inverse = lax.rsqrt(jnp.mean(wide * wide, axis=-1, keepdims=True) + 1e-05)
        normed = (wide * inverse * gain_ref[...]).astype(jnp.bfloat16)
        out_ref[first + at : first + at + step] = normed


def forward_heads(batches, weight, helds, start, gain, saved):
    rows, width = batches[0][0].shape
    cores = len(batches[0])
    length = rows * cores
    wide = GROUP * length
    flat = [part for parts in batches for part in parts]
    depth = divisor(width, 1024)
    steps = width // depth
    units = sum(held.shape[0] for held in helds) // steps if helds else weight.shape[1] // UNIT

    def kernel(ins, outs, block, normed_ref):
        for index, ref in enumerate(ins[2 : 2 + len(flat)]):
            normalize_rows(ref, ins[1], normed_ref, index * rows)
        masked = later_keys(length, ins[0][0])
        if saved is not None:
            rolled = rolled_rows(ins[-1], ins[0][0], cores)
            for unit in range(units):
                qkv = rolled(slice(unit * UNIT, (unit + 1) * UNIT))
                outs[-1][unit * wide : (unit + 1) * wide] = probabilities(
                    stacked_heads(qkv), head_columns(qkv, GROUP), masked
                )
        for unit in range(units):
            total = None
            for step in range(steps):
                left = normed_ref[:, step * depth : (step + 1) * depth]
                product = mxu(left, block(unit * steps + step), 1, 0)
                total = product if total is None else total + product
            total = total.astype(jnp.bfloat16)
            for index in range(len(batches)):
                qkv = total[index * length : (index + 1) * length]
                attend_unit(qkv, masked, outs[index], unit * GROUP * HD)

    blocks = []
    if not helds:
        blocks = [
            (pl.ds(step * depth, depth), pl.ds(unit * UNIT, UNIT))
            for unit in range(units)
            for step in range(steps)
        ]
    flops = 2 * length * len(batches) * width * units * UNIT
    outs = [(length, units * GROUP * HD) for _ in batches]
    temps = [pltpu.VMEM((length * len(batches), width), jnp.bfloat16)]
    args = [start, gain] + flat
    fetch = ()
    if saved is not None:
        args.append(saved)
        fetch = (1, 2, len(args) - 1)
        outs.append(jax.ShapeDtypeStruct((units * wide, length), jnp.float32))
    keep = not helds
    return call(kernel, args, weight, helds, outs, blocks, keep, flops, temps, fetch)


def column_parts(depth):
    first = GROUP * HD
    return [(0, first), (first, depth)] if depth > first else [(0, depth)]


def head_terms(pieces, weight, whole):
    rows, columns = pieces[0][0].shape
    length = rows * len(pieces[0])
    depth = weight.shape[0]
    flat = [part for parts in pieces for part in parts]
    blocks = row_blocks(depth, columns, 768)
    block = depth // len(blocks)
    places = [(k, 0, depth) for k in range(whole)]
    for first, last in column_parts(depth):
        places += [(k, first, last) for k in range(whole, len(pieces))]

    def kernel(ins, outs, loaded):
        left = jnp.concatenate([ref[...] for ref in ins], axis=0)
        for step in range(len(blocks)):
            product = mxu(left, loaded(step), 1, 1).astype(jnp.bfloat16)
            at = step * block
            for (k, first, last), out_ref in zip(places, outs):
                if first <= at < last:
                    out_ref[:, at - first : at - first + block] = product[
                        k * length : (k + 1) * length
                    ]

    outs = [(length, last - first) for _, first, last in places]
    flops = 2 * len(pieces) * length * depth * columns
    *terms, held = call(kernel, flat, weight, [], outs, blocks, True, flops)
    return terms, held


def project(heads, held, cores):
    length = heads[0].shape[0]
    count, (steps, block, columns) = len(heads), held.shape
    rows = length // cores

    def kernel(ins, outs, held_block):
        total = None
        for step in range(steps):
            at = slice(step * block, (step + 1) * block)
            left = jnp.concatenate([ref[:, at] for ref in ins], axis=0)
            product = mxu(left, held_block(step), 1, 0)
            total = product if total is None else total + product
        total = total.astype(jnp.bfloat16)
        for core, out_ref in enumerate(outs):
            for index in range(count):
                at = index * length + core * rows
                out_ref[index * rows : (index + 1) * rows] = total[at : at + rows]

    outs = [(count * rows, columns) for _ in range(cores)]
    flops = 2 * count * length * steps * block * columns
    return call(kernel, heads, None, [held], outs, [], False, flops)


def rolled_rows(ref, start, cores):
    length = ref.shape[0]
    rows = length // cores
    ranges = []
    for core in range(cores):
        at = start + core * rows
        at = jnp.where(at >= length, at - length, at)
        ranges.append(pl.ds(pl.multiple_of(at, rows), rows))
    return lambda columns: jnp.concatenate([ref[part, columns] for part in ranges], axis=0)


def back_units(start_ref, qkv_ref, probs_ref, own_ref, landed, grad_ref, units, cores):
    high = GROUP * qkv_ref.shape[0]
    saved = rolled_rows(qkv_ref, start_ref[0], cores)
    wide = GROUP * HD
    for place, unit in enumerate(units):
        grads = own_ref[:, unit * wide : (unit + 1) * wide].astype(jnp.float32)
        for ref in landed:
            grads = grads + ref[:, place * wide : (place + 1) * wide].astype(jnp.float32)
        attend_back_unit(
            saved(slice(unit * UNIT, (unit + 1) * UNIT)),
            grads.astype(jnp.bfloat16),
            probs_ref[unit * high : (unit + 1) * high],
            grad_ref,
            place * UNIT,
        )


def back_product(grad_ref, block, units, step, steps):
    total = None
    for place, unit in enumerate(units):
        grads = grad_ref[:, place * UNIT : (place + 1) * UNIT]
        product = mxu(grads, block(unit * steps + step), 1, 1)
        total = product if total is None else total + product
    return total


def back_early(qkv, probs, own, landed, helds, start, cores, units, steps):
    length = qkv.shape[0]
    depth = helds[0].shape[1]

    def kernel(ins, outs, block):
        back_units(*ins[:4], ins[4:], outs[0], units, cores)
        for step in range(steps):
            outs[1][:, step * depth : (step + 1) * depth] = back_product(
                outs[0], block, units, step, steps
            )

    wide = len(units) * UNIT
    outs = [(length, wide), jax.ShapeDtypeStruct((length, steps * depth), jnp.float32)]
    flops = 2 * length * wide * steps * depth
    args = [start, qkv, probs, own] + landed
    return call(kernel, args, None, helds, outs, [], False, flops)[1]


def back_columns(grad_ref, early, outs, block, units, picked, steps, depth):
    rows = grad_ref.shape[0] // len(outs)
    for place, step in enumerate(picked):
        total = back_product(grad_ref, block, units, step, steps)
        for ref in early:
            total = total + ref[:, step * depth : (step + 1) * depth]
        total = total.astype(jnp.bfloat16)
        for core, out_ref in enumerate(outs):
            out_ref[:, place * depth : (place + 1) * depth] = total[
                core * rows : (core + 1) * rows
            ]


def back_first(qkv, probs, own, landed, early, helds, start, cores, units, picked, steps):
    length = qkv.shape[0]
    rows = length // cores
    depth = helds[0].shape[1]
    count = 4 + len(landed)

    def kernel(ins, outs, block):
        back_units(*ins[:4], ins[4:count], outs[0], units, cores)
        back_columns(outs[0], ins[count:], outs[1:], block, units, picked, steps, depth)

    wide = len(units) * UNIT
    columns = len(picked) * depth
    outs = [(length, wide)] + [(rows, columns) for _ in range(cores)]
    flops = 2 * length * wide * columns
    args = [start, qkv, probs, own] + landed + early
    results = call(kernel, args, None, helds, outs, [], False, flops)
    return results[0], results[1:]


def back_rest(grad_qkv, early, helds, cores, units, picked, steps):
    length, wide = grad_qkv.shape
    depth = helds[0].shape[1]

    def kernel(ins, outs, block):
        back_columns(ins[0], ins[1:], outs, block, units, picked, steps, depth)

    columns = len(picked) * depth
    outs = [(length // cores, columns) for _ in range(cores)]
    flops = 2 * length * wide * columns
    return call(kernel, [grad_qkv] + early, None, helds, outs, [], False, flops)


def norm_back(inputs, grad_rows, parts):
    rows, _ = inputs.shape
    step = 16 if rows % 16 == 0 else rows

    def kernel(inputs_ref, grad_ref, *refs):
        *part_refs, out_ref = refs
        for at in range(0, rows, step):
            wide = inputs_ref[at : at + step].astype(jnp.float32)
            scaled = [ref[at : at + step].astype(jnp.float32) for ref in part_refs]
            scaled = jnp.concatenate(scaled, axis=1)
            inverse = lax.rsqrt(jnp.mean(wide * wide, axis=-1, keepdims=True) + 1e-05)
            middle = jnp.mean(wide * scaled, axis=-1, keepdims=True)
            result = (
                grad_ref[at : at + step].astype(jnp.float32)
                + inverse * scaled
                - wide * (inverse * inverse * inverse * middle)
            )
            out_ref[at : at + step] = result.astype(jnp.bfloat16)

    return pl.pallas_call(
        kernel,
        in_specs=[LOCAL for _ in range(2 + len(parts))],
        out_specs=LOCAL,
        out_shape=jax.ShapeDtypeStruct(inputs.shape, jnp.bfloat16),
        compiler_params=pltpu.CompilerParams(vmem_limit_bytes=8 << 20),
        name="norm_back",
    )(inputs, grad_rows, *parts)


def per_device(x_fwd, x_bwd, grad_out, saved_qkv, norm_gain, w_qkv, w_out):
    return window(
        x_fwd[0, 0],
        x_bwd[0, 0],
        grad_out[0, 0],
        saved_qkv[0, 0],
        norm_gain,
        w_qkv[0],
        w_out[0],
    )


def window(fwd_rows, bwd_rows, grad_rows, qkv_saved, gain_row, weight_qkv, weight_out):
    rows, width = fwd_rows.shape
    cores = lax.axis_size("tensor")
    replicas = lax.axis_size("dp")
    columns = weight_out.shape[1]
    words = jnp.full((1,), lax.axis_index("tensor") * rows, jnp.int32)

    def columns_of(step):
        return jnp.bitwise_xor(lax.axis_index("dp"), step) * columns

    if replicas != 4:
        raise ValueError("dp size")

    def grad_piece(step):
        return lax.dynamic_slice_in_dim(grad_rows, columns_of(step), columns, axis=1)

    moved = [grad_piece(0)]
    moved += [over_dp(grad_piece(step), step) for step in range(1, replicas)]

    far_rows = over_dp(fwd_rows, 3)
    near_rows = over_dp(fwd_rows, 1)
    own_parts = blocks_of_cores(fwd_rows)
    own_heads, probs, *helds = forward_heads(
        [own_parts], weight_qkv, [], words, gain_row, qkv_saved
    )
    near_parts = blocks_of_cores(near_rows)
    far_parts = blocks_of_cores(far_rows)
    near_heads, far_heads = forward_heads(
        [near_parts, far_parts], None, helds, words, gain_row, None
    )
    last_heads = over_dp(far_heads, 1)

    exchanged = [blocks_of_cores(piece) for piece in moved]
    (own, *rest), held_out = head_terms(exchanged, weight_out, 1)
    landed = []
    for index in range(len(rest) // 3):
        near, far, relay = rest[3 * index : 3 * index + 3]
        near = over_dp(near, 1)
        relay = over_dp(relay, 1)
        far = (far.astype(jnp.float32) + relay.astype(jnp.float32)).astype(jnp.bfloat16)
        landed.append([near, over_dp(far, 2)])

    fwd_prev = over_pipe(fwd_rows, 1)
    bwd_next = over_pipe(bwd_rows, -1)
    grad_next = over_pipe(grad_rows, -1)

    depth = helds[0].shape[1]
    steps = width // depth
    some = steps - max(1, steps // 4)
    some = steps - max(1, steps // 2)
    some = steps - max(1, steps // 2)
    first, rest = range(some), range(some, steps)
    half = len(first) * depth
    units = range(qkv_saved.shape[1] // UNIT)
    early = []
    if len(landed) > 1:
        shares = (qkv_saved, probs, own, landed[0], helds, words, cores, units[:1], steps)
        early = [back_early(*shares)]
        units = units[1:]
    shares = (qkv_saved, probs, own, landed[-1], early, helds, words, cores, units, first, steps)
    grad_qkv, (keep, *sends) = back_first(*shares)
    scaled = sum_over_cores(keep, sends) * gain_row[:, :half]
    arrived = [over_pipe(scaled.astype(jnp.bfloat16), -1)]
    keep, *sends = back_rest(grad_qkv, early, helds, cores, units, rest, steps)
    scaled = sum_over_cores(keep, sends) * gain_row[:, half:]
    arrived.append(over_pipe(scaled.astype(jnp.bfloat16), -1))
    grad_input = norm_back(bwd_next, grad_next, arrived)

    pieces = []
    groups = (((0,), [own_heads]), ((1, 3), [near_heads, far_heads]), ((2,), [last_heads]))
    for group, heads in groups:
        keep, *sends = project(heads, held_out, cores)
        summed = sum_over_cores(keep, sends).astype(jnp.bfloat16)
        for index, step in enumerate(group):
            piece = lax.ppermute(
                summed[index * rows : (index + 1) * rows],
                ("pipe", "dp"),
                cross_pairs(step, 1),
            )
            pieces.append((step, piece))
    output = fwd_prev
    for step, piece in reversed(pieces):
        at = columns_of(step)
        part = lax.dynamic_slice_in_dim(fwd_prev, at, columns, axis=1).astype(jnp.float32)
        part = (part + piece.astype(jnp.float32)).astype(jnp.bfloat16)
        output = lax.dynamic_update_slice_in_dim(output, part, at, axis=1)
    return (output[None, None], grad_input[None, None])


def solution(mesh):
    return jax.shard_map(
        per_device,
        mesh=mesh,
        in_specs=(
            P("pipe", "dp", "tensor", None),
            P("pipe", "dp", "tensor", None),
            P("pipe", "dp", "tensor", None),
            P("pipe", "dp", None, "tensor"),
            P("pipe", None),
            P("pipe", None, "tensor"),
            P("pipe", "tensor", "dp"),
        ),
        out_specs=(P("pipe", "dp", "tensor", None), P("pipe", "dp", "tensor", None)),
        check_vma=False,
    )
```
